32 devices in a mesh: section: 2 (over core), ha: 4 (over z), wa: 4 (over y, x).
Axes of the slice: x: 2, y: 2, z: 4, core: 2. Of those that a mesh axis runs over, the one named last changes fastest.
Arguments:
- queries: bfloat16 [2, 1, 32, 64, 1536], P('section', None, 'ha', 'wa'), may hold values from -85 to 85
- keys: bfloat16 [2, 1, 32, 64, 1536], P('section', None, 'ha', 'wa'), may hold values from -4.5 to 4.5
- values: bfloat16 [2, 1, 32, 64, 1536], P('section', None, 'ha', 'wa'), may hold values from -6 to 6
- cotangent: bfloat16 [2, 1, 32, 64, 1536], P('section', None, 'ha', 'wa'), may hold values from -6 to 6
- upstream: bfloat16 [2, 1, 32, 64, 1536], P('section', None, 'ha', 'wa'), may hold values from -6 to 6
- block_mask: int32 [2, 4, 8, 9], P('section', 'ha', 'wa'), may hold values from 0 to 1, as said below
Outputs:
- grad_queries: bfloat16 [2, 1, 32, 64, 1536], P('section', None, 'ha', 'wa')
- grad_keys: bfloat16 [2, 1, 32, 64, 1536], P('section', None, 'ha', 'wa')
- grad_values: bfloat16 [2, 1, 32, 64, 1536], P('section', None, 'ha', 'wa')
The draws below stay inside these ranges and needn't reach their ends.
Inputs may be any that keep to these rules, and one draw needn't show every extreme that they name: `block_mask`: entry 4, the tile's own block, is always 1.
All inputs are finite; a program needn't handle non-finite values.
Results may differ from the reference program's by a relative error of at most 0.0068.
Values may be sent and summed in bfloat16 or wider, within the bound.
A program may use at most 64 MiB of HBM per device.

```python
import jax
import jax.numpy as jnp
from jax import lax

HEADS = 12
HEAD_DIM = 128
TILE = 8
SPAN_TILES = 2
FRAMES = 1
SECTIONS = 2
TILE_ROWS = 4
TILE_COLS = 8
HEIGHT = 32
WIDTH = 64
CHANNELS = 1536


def pair_fields(key):
    base_key = jax.random.fold_in(key, 5)
    key_a, key_b = jax.random.split(base_key, 2)
    field_shape = (SECTIONS, FRAMES, HEIGHT, WIDTH, CHANNELS)
    key_field = jnp.clip(jax.random.normal(key_b, field_shape, jnp.float32), -4.0, 4.0)
    query_field = jnp.clip(jax.random.normal(key_a, field_shape, jnp.float32), -4.0, 4.0)
    return (query_field, key_field)


def draw_queries(key, part):
    query_field, key_field = pair_fields(key)
    return query_field.astype(jnp.bfloat16)


def draw_keys(key, part):
    query_field, key_field = pair_fields(key)
    return key_field.astype(jnp.bfloat16)


def draw_block_mask(key, part):
    mask_key = jax.random.fold_in(key, 11)
    picks = jax.random.randint(mask_key, (SECTIONS, TILE_ROWS, TILE_COLS, 9), 0, 4)
    center = jnp.arange(9, dtype=jnp.int32) == 4
    return jnp.where(center[None, None, None, :], 1, (picks > 0).astype(jnp.int32)).astype(jnp.int32)


def block_levels(own_key, dims, cuts, smallest, high):
    def one(dim, shards_of):
        heights = jax.random.uniform(jax.random.fold_in(jax.random.fold_in(own_key, 6), dim), (shards_of,), jnp.float32, smallest / len(cuts), high / len(cuts))
        return jnp.repeat(jnp.exp(heights), dims[dim] // shards_of).reshape((-1,) + (1,) * (len(dims) - dim - 1))

    factor_of = one(*cuts[0])
    for cut in cuts[1:]:
        factor_of = factor_of * one(*cut)
    return factor_of


def noise(own_key, extent, width, limit, cuts=(), held_as=jnp.bfloat16):
    level = block_levels(own_key, extent, cuts, -0.22, 0.18) if cuts else 1.0
    result = jax.random.normal(own_key, extent, jnp.float32) * width * level
    return jnp.minimum(jnp.maximum(result, -limit), limit).astype(held_as)


def setup_inputs(seed: int = 0) -> dict:
    splits = jax.random.split(jax.random.key(seed), 7)
    return {
        "queries": draw_queries(jax.random.fold_in(splits[6], 71), 0),
        "keys": draw_keys(jax.random.fold_in(splits[6], 71), 0),
        "values": noise(splits[2], (SECTIONS, FRAMES, HEIGHT, WIDTH, CHANNELS), 1.0, 6.0, ((0, 2), (2, 4), (3, 4))),
        "cotangent": noise(splits[3], (SECTIONS, FRAMES, HEIGHT, WIDTH, CHANNELS), 1.0, 6.0, ((0, 2), (2, 4), (3, 4))),
        "upstream": noise(splits[4], (SECTIONS, FRAMES, HEIGHT, WIDTH, CHANNELS), 1.0, 6.0, ((0, 2), (2, 4), (3, 4))),
        "block_mask": draw_block_mask(jax.random.fold_in(splits[6], 71), 0),
    }


def window_live(mask_table, tile_row, tile_col, grid_height, grid_width):
    box_span = 3 * TILE
    offsets = jnp.arange(box_span, dtype=jnp.int32)
    rows_at = tile_row * TILE - TILE + offsets
    cols_at = tile_col * TILE - TILE + offsets
    part_of = offsets // TILE
    thirds = jnp.arange(3, dtype=jnp.int32)
    part_hot = (part_of[:, None] == thirds[None, :]).astype(jnp.float32)
    grid_mask = mask_table.reshape(3, 3).astype(jnp.float32)
    allowed = jnp.dot(jnp.dot(part_hot, grid_mask), part_hot.T)
    inside_rows = (rows_at >= 0) & (rows_at < grid_height)
    inside_cols = (cols_at >= 0) & (cols_at < grid_width)
    return (allowed > 0.5) & inside_rows[:, None] & inside_cols[None, :]


def tile_grads(query_rows, key_rows, value_rows, grad_rows, live_keys):
    inv_root = HEAD_DIM ** -0.5
    query_wide = query_rows.astype(jnp.float32)
    key_wide = key_rows.astype(jnp.float32)
    value_wide = value_rows.astype(jnp.float32)
    grad_wide = grad_rows.astype(jnp.float32)
    scores = jnp.einsum("qhd,khd->hqk", query_wide, key_wide) * inv_root
    scores = jnp.where(live_keys[None, None, :], scores, -jnp.inf)
    row_max = jnp.max(scores, axis=2, keepdims=True)
    weights = jnp.exp(scores - row_max)
    softmax_probs = weights / jnp.sum(weights, axis=2, keepdims=True)
    probs_low = softmax_probs.astype(jnp.bfloat16)
    probs_wide = probs_low.astype(jnp.float32)
    attended = jnp.einsum("hqk,khd->qhd", probs_wide, value_wide)
    deltas = jnp.sum(grad_wide * attended, axis=2)
    grad_probs = jnp.einsum("qhd,khd->hqk", grad_wide, value_wide)
    grad_scores = (softmax_probs * (grad_probs - deltas.T[:, :, None]) * inv_root).astype(jnp.bfloat16)
    scores_wide = grad_scores.astype(jnp.float32)
    grad_query = jnp.einsum("hqk,khd->qhd", scores_wide, key_wide)
    grad_key = jnp.einsum("hqk,qhd->khd", scores_wide, query_wide)
    grad_value = jnp.einsum("hqk,qhd->khd", probs_wide, grad_wide)
    return grad_query, grad_key, grad_value


def rounded(values_in):
    low = lax.optimization_barrier(values_in.astype(jnp.bfloat16))
    return low.astype(jnp.float32)


def section_grads(section_queries, section_keys, section_values, section_grad, section_mask):
    frames_n, grid_height, grid_width, chan_count = section_queries.shape
    box_span = 3 * TILE
    own_width = SPAN_TILES * TILE
    ext_width = own_width + 2 * TILE
    pair_rows_n = grid_height // TILE
    pair_cols_n = grid_width // own_width
    tile_tokens = frames_n * TILE * TILE
    box_rows = frames_n * box_span * box_span
    padded_kv = jnp.pad(jnp.concatenate((section_keys, section_values), axis=3), ((0, 0), (TILE, TILE), (TILE, TILE), (0, 0)))
    zero_idx = jnp.int32(0)

    def one_pair(pair_index):
        pair_row = (pair_index // pair_cols_n).astype(jnp.int32)
        pair_col = (pair_index % pair_cols_n).astype(jnp.int32)
        start_row = (pair_row * TILE).astype(jnp.int32)
        start_col = (pair_col * own_width).astype(jnp.int32)
        region = lax.dynamic_slice(padded_kv, (zero_idx, start_row, start_col, zero_idx), (frames_n, box_span, ext_width, 2 * chan_count))
        query_block = lax.dynamic_slice(section_queries, (zero_idx, start_row, start_col, zero_idx), (frames_n, TILE, own_width, chan_count))
        grad_block = lax.dynamic_slice(section_grad, (zero_idx, start_row, start_col, zero_idx), (frames_n, TILE, own_width, chan_count))
        ext_grads = jnp.zeros((frames_n, box_span, ext_width, 2 * chan_count), jnp.float32)
        query_parts = []
        for tile_at in range(SPAN_TILES):
            tile_col = (pair_col * SPAN_TILES + tile_at).astype(jnp.int32)
            mask_row = lax.dynamic_slice(section_mask, (pair_row, tile_col, zero_idx), (1, 1, 9)).reshape(9)
            live_cells = window_live(mask_row, pair_row, tile_col, grid_height, grid_width)
            live_keys = jnp.broadcast_to(live_cells[None], (frames_n, box_span, box_span)).reshape(box_rows)
            start = tile_at * TILE
            box_tile = region[:, :, start:start + box_span, :]
            grad_query, grad_key, grad_value = tile_grads(
                query_block[:, :, start:start + TILE, :].reshape(tile_tokens, HEADS, HEAD_DIM),
                box_tile[..., :chan_count].reshape(box_rows, HEADS, HEAD_DIM),
                box_tile[..., chan_count:].reshape(box_rows, HEADS, HEAD_DIM),
                grad_block[:, :, start:start + TILE, :].reshape(tile_tokens, HEADS, HEAD_DIM),
                live_keys)
            box_grads = jnp.concatenate((grad_key.reshape(frames_n, box_span, box_span, chan_count),
                                         grad_value.reshape(frames_n, box_span, box_span, chan_count)), axis=3)
            ext_grads = ext_grads.at[:, :, start:start + box_span, :].add(box_grads)
            query_parts.append(grad_query.reshape(frames_n, TILE, TILE, chan_count).astype(jnp.bfloat16))
        center = ext_grads[:, :, TILE:ext_width - TILE, :]
        rims = jnp.concatenate([ext_grads[:, :, :TILE, :], ext_grads[:, :, ext_width - TILE:, :]], axis=2).astype(jnp.bfloat16)
        return jnp.concatenate(query_parts, axis=2), center, rims

    query_pairs, centers, rims = lax.map(one_pair, jnp.arange(pair_rows_n * pair_cols_n, dtype=jnp.int32))
    centers = centers.reshape(pair_rows_n, pair_cols_n, frames_n, box_span, own_width, 2 * chan_count)
    rims = rims.reshape(pair_rows_n, pair_cols_n, frames_n, box_span, 2 * TILE, 2 * chan_count).astype(jnp.float32)
    left_parts = rims[..., :TILE, :]
    right_parts = rims[..., TILE:, :]
    col_zero = jnp.zeros_like(right_parts[:, :1])
    from_before = jnp.concatenate([col_zero, right_parts[:, :pair_cols_n - 1]], axis=1)
    from_after = jnp.concatenate([left_parts[:, 1:], col_zero], axis=1)
    gap_shape = list(from_before.shape)
    gap_shape[4] = own_width - 2 * TILE
    col_gap = jnp.zeros(gap_shape, jnp.float32)
    col_folded = centers + jnp.concatenate([from_before, col_gap, from_after], axis=4)
    lower = rounded(col_folded[:, :, :, :TILE])
    upper = rounded(col_folded[:, :, :, 2 * TILE:])
    row_zero = jnp.zeros_like(lower[:1])
    from_above = jnp.concatenate([row_zero, upper[:pair_rows_n - 1]], axis=0)
    from_below = jnp.concatenate([lower[1:], row_zero], axis=0)
    folded_all = (col_folded[:, :, :, TILE:2 * TILE] + from_above + from_below).astype(jnp.bfloat16)
    folded_all = folded_all.transpose(2, 0, 3, 1, 4, 5).reshape(frames_n, grid_height, grid_width, 2 * chan_count)
    query_pairs = query_pairs.reshape(pair_rows_n, pair_cols_n, frames_n, TILE, own_width, chan_count)
    query_grid = query_pairs.transpose(2, 0, 3, 1, 4, 5).reshape(frames_n, grid_height, grid_width, chan_count)
    return query_grid, folded_all[..., :chan_count], folded_all[..., chan_count:]


def reference(queries, keys, values, cotangent, upstream, block_mask):
    handed = jnp.concatenate([upstream[1:], jnp.zeros_like(upstream[:1])], axis=0)
    grad_out = (cotangent.astype(jnp.float32) + handed.astype(jnp.float32)).astype(jnp.bfloat16)

    def per_section(slices):
        return section_grads(slices[0], slices[1], slices[2], slices[3], slices[4])

    grad_queries, grad_keys, grad_values = lax.map(per_section, (queries, keys, values, grad_out, block_mask))
    return (grad_queries, grad_keys, grad_values)
```

```python
import functools

import jax
import jax.numpy as jnp
from jax import lax
from jax.experimental import pallas as pl
from jax.experimental.pallas import tpu as pltpu
from jax.sharding import PartitionSpec as P

HEADS = 12
HEAD_DIM = 128
TILE = 8


NEG = -1e30
LANES = 128
GROUP = 2
SPAN = 4
AHEAD = 3
LAG = 3
MESH_ID = pl.DeviceIdType.MESH


def relay_kernel(
    sections, rows_n, cols_n,
    q_hbm, k_hbm, v_hbm, c_hbm, u_hbm, mask_hbm,
    oq_ref, ok_ref, ov_ref,
    q_ref, k_ref, v_ref, c_ref, mask_ref, handed,
    qb, gb, kb, vb, k_send, v_send, bias_send, bias,
    weights, grads, xs1, xr1, xs2, xr2,
    dq_own, dq_send, dq_recv, dk_own, dv_own, dk_send, dv_send, dk_recv, dv_recv, via_v, via_dv,
    load_sem, sec_sem, bias_sem, send_q, send_g, send_dq, send_k, send_v, send_dk, send_dv,
    send_x1, send_x2, send_via, recv_q, recv_g, recv_dq, recv_k, recv_v, recv_dk, recv_dv,
    recv_x1, recv_x2, recv_via_v, recv_via_dv,
):
    f32, bf16 = jnp.float32, jnp.bfloat16
    sec = lax.axis_index("section")
    row = lax.axis_index("ha")
    col = lax.axis_index("wa")
    groups = HEADS // GROUP
    spans = HEADS // SPAN
    per_span = SPAN // GROUP
    inv_root = HEAD_DIM ** (-0.5)
    scale = inv_root * 1.4426950408889634
    has_up, has_down = row > 0, row < rows_n - 1
    has_up2, has_down2 = row > 1, row < rows_n - 2
    has_left, has_right = col > 0, col < cols_n - 1
    detour = cols_n == 4

    loads = [
        pltpu.make_async_copy(src, dst, load_sem.at[n])
        for n, (src, dst) in enumerate(
            ((q_hbm, q_ref), (k_hbm, k_ref), (v_hbm, v_ref), (mask_hbm, mask_ref), (c_hbm, c_ref))
        )
    ]
    for load in loads:
        load.start()

    barrier = pltpu.get_barrier_semaphore()
    greeted = [
        (has_up, {"ha": row - 1}),
        (has_down, {"ha": row + 1}),
        (has_up2, {"ha": row - 2}),
        (has_down2, {"ha": row + 2}),
        (has_left, {"wa": col - 1}),
        (has_right, {"wa": col + 1}),
        (sec > 0, {"section": sec - 1}),
        (sec < sections - 1, {"section": sec + 1}),
    ]
    if detour:
        greeted.append((col >= 0, {"wa": lax.rem(col + 2, 4)}))
    expected = jnp.int32(0)
    for cond, dev in greeted:
        @pl.when(cond)
        def _(dev=dev):
            pl.semaphore_signal(barrier, inc=1, device_id=dev, device_id_type=MESH_ID)

        expected = expected + cond.astype(jnp.int32)

    def remote(src, dst, send, recv, dev):
        return pltpu.make_async_remote_copy(
            src_ref=src, dst_ref=dst, send_sem=send, recv_sem=recv,
            device_id=dev, device_id_type=MESH_ID,
        )

    vertical = ((has_up, has_down, {"ha": row - 1}), (has_down, has_up, {"ha": row + 1}))
    sideways = ((has_left, has_right, {"wa": col - 1}), (has_right, has_left, {"wa": col + 1}))

    def slot_rows(d):
        return pl.ds(256 - 256 * d, 128)

    def halo_rows(side):
        return pl.ds(192 - 64 * side, 64)

    sec_copy = remote(u_hbm, handed, sec_sem.at[0], sec_sem.at[1], {"section": sec - 1})

    def bias_copy(d):
        return remote(
            bias_send.at[2 * d], bias.at[2 - 2 * d], bias_sem.at[0, d], bias_sem.at[1, d],
            vertical[d][2],
        )

    def rows_copy(buf, send, recv, d, heads, g):
        return remote(
            buf.at[heads, pl.ds(128, 128)], buf.at[heads, slot_rows(d)],
            send.at[d], recv.at[d, g], vertical[d][2],
        )

    def q_copy(d, g):
        return rows_copy(qb, send_q, recv_q, d, pl.ds(g * GROUP, GROUP), g)

    def g_copy(d, g):
        return rows_copy(gb, send_g, recv_g, d, pl.ds(g * GROUP, GROUP), g)

    def dq_copy(d, g, heads):
        return remote(
            dq_send.at[d, heads], dq_recv.at[1 - d, heads],
            send_dq.at[d], recv_dq.at[1 - d, g], vertical[d][2],
        )

    def k_copy(side, heads, s):
        return remote(
            k_send.at[side, heads], kb.at[heads, halo_rows(side)],
            send_k.at[side], recv_k.at[side, s], sideways[side][2],
        )

    def v_copy(side, heads, s):
        return remote(
            v_send.at[side, heads], vb.at[heads, halo_rows(side)],
            send_v.at[side], recv_v.at[side, s], sideways[side][2],
        )

    def dk_copy(side, heads, s):
        return remote(
            dk_send.at[side, heads], dk_recv.at[1 - side, heads],
            send_dk.at[side], recv_dk.at[1 - side, s], sideways[side][2],
        )

    def dv_copy(side, heads, s):
        return remote(
            dv_send.at[side, heads], dv_recv.at[1 - side, heads],
            send_dv.at[side], recv_dv.at[1 - side, s], sideways[side][2],
        )

    def via_source(side):
        return col == (2, 1)[side]

    def via_holder(side):
        return col == (0, 3)[side]

    def via_v_in(side, heads, s):
        return remote(
            v_send.at[side, heads], via_v.at[heads], send_v.at[side], recv_via_v.at[s],
            {"wa": jnp.int32((0, 3)[side])},
        )

    def via_v_out(side, heads, s):
        return remote(
            via_v.at[heads], vb.at[heads, halo_rows(side)], send_via.at[0], recv_v.at[side, s],
            {"wa": jnp.int32((1, 2)[side])},
        )

    def via_dv_in(side, heads, g):
        return remote(
            dv_send.at[side, heads], via_dv.at[heads], send_dv.at[side], recv_via_dv.at[g],
            {"wa": jnp.int32((0, 3)[side])},
        )

    def via_dv_out(side, heads, s):
        return remote(
            via_dv.at[heads], dv_recv.at[1 - side, heads], send_via.at[1],
            recv_dv.at[1 - side, s], {"wa": jnp.int32((1, 2)[side])},
        )

    stat_moves = (
        (has_up, has_down, {"ha": row - 1}, pl.ds(0, 2), pl.ds(2, 2)),
        (has_down, has_up, {"ha": row + 1}, pl.ds(1, 2), pl.ds(0, 2)),
        (has_up2, has_down2, {"ha": row - 2}, pl.ds(0, 1), pl.ds(5, 1)),
        (has_down2, has_up2, {"ha": row + 2}, pl.ds(2, 1), pl.ds(4, 1)),
    )

    def stat_copy(xs, xr, send, recv, m, g):
        _, _, dev, mine, theirs = stat_moves[m]
        return remote(xs.at[g, mine], xr.at[g, theirs], send.at[m], recv.at[m, g], dev)

    def stat_start(xs, xr, send, recv, g):
        for m in range(4):
            @pl.when(stat_moves[m][0])
            def _(m=m):
                stat_copy(xs, xr, send, recv, m, g).start()

    def stat_wait(xs, xr, send, recv, g):
        for m in range(4):
            @pl.when(stat_moves[m][1])
            def _(m=m):
                stat_copy(xs, xr, send, recv, m, g).wait_recv()

    def head_cols(head):
        return pl.ds(pl.multiple_of(head * LANES, LANES), LANES)

    for cond, at in ((row == 0, 0), (row == rows_n - 1, 256)):
        @pl.when(cond)
        def _(at=at):
            bias[2 * at // 256] = jnp.zeros((4, 8, LANES), f32)

            @pl.loop(0, HEADS)
            def _(h):
                qb[h, pl.ds(at, 128)] = jnp.zeros((128, LANES), bf16)
                gb[h, pl.ds(at, 128)] = jnp.zeros((128, LANES), bf16)
                dq_recv[at // 256, h] = jnp.zeros((128, LANES), bf16)

    for cond, side in ((col == 0, 0), (col == cols_n - 1, 1)):
        @pl.when(cond)
        def _(side=side):
            @pl.loop(0, HEADS)
            def _(h):
                kb[h, pl.ds(128 + 64 * side, 64)] = jnp.zeros((64, LANES), bf16)
                vb[h, pl.ds(128 + 64 * side, 64)] = jnp.zeros((64, LANES), bf16)
                dk_recv[side, h] = jnp.zeros((64, LANES), bf16)
                dv_recv[side, h] = jnp.zeros((64, LANES), bf16)

    no_stat = jnp.where(lax.broadcasted_iota(jnp.int32, (8, LANES), 0) < GROUP, NEG, 0.0).astype(f32)
    for cond, pieces in (
        (row == 0, (0, 1)), (row < 2, (4,)),
        (row == rows_n - 1, (2, 3)), (row > rows_n - 3, (5,)),
    ):
        @pl.when(cond)
        def _(pieces=pieces):
            for g in range(groups):
                for piece in pieces:
                    xr1[g, piece] = no_stat
                    xr2[g, piece] = jnp.zeros((8, LANES), f32)

    loads[0].wait()

    @pl.loop(0, HEADS)
    def _(h):
        qb[h, pl.ds(128, 128)] = q_ref[:, head_cols(h)]

    def split(block):
        tiles = block.astype(f32).reshape(8, 2, 8, LANES)
        return [tiles[:, t].reshape(64, LANES).astype(bf16) for t in range(2)]

    for load, ref, buf, send in ((1, k_ref, kb, k_send), (2, v_ref, vb, v_send)):
        loads[load].wait()

        @pl.loop(0, HEADS)
        def _(h, ref=ref, buf=buf, send=send):
            block = ref[:, head_cols(h)]
            buf[h, pl.ds(0, 128)] = block
            for side, part in enumerate(split(block)):
                send[side, h] = part

    loads[3].wait()
    lane = lax.broadcasted_iota(jnp.int32, (8, LANES), 1)
    first_tile = lax.rem(lane // TILE, 2) == 0
    dead = jnp.int32(0)
    for i in range(3):
        entry = [[mask_ref[t, 3 * i + j] for j in range(3)] for t in range(2)]
        left = jnp.where(has_left, 1, 0)
        right = jnp.where(has_right, 1, 0)
        for n, (first, second) in enumerate((
            (entry[0][1], entry[1][0]),
            (entry[0][2], entry[1][1]),
            (entry[0][0] * left, dead),
            (dead, entry[1][2] * right),
        )):
            seen = jnp.where(first_tile, first, second)
            bias_send[i, n] = jnp.where(seen > 0, 0.0, NEG).astype(f32)
    bias[1] = bias_send[1]

    pl.semaphore_wait(barrier, expected)

    @pl.when(sec > 0)
    def _():
        sec_copy.start()

    for d in range(2):
        @pl.when(vertical[d][0])
        def _(d=d):
            bias_copy(d).start()

    def issue(copy, g):
        for d in range(2):
            @pl.when(vertical[d][0])
            def _(d=d):
                copy(d, g).start()

    for g in range(AHEAD):
        issue(q_copy, g)

    for s in range(spans):
        for side in range(2):
            @pl.when(sideways[side][0])
            def _(side=side, s=s):
                k_copy(side, pl.ds(s * SPAN, SPAN), s).start()

    for s in range(spans):
        for side in range(2):
            heads = pl.ds(s * SPAN, SPAN)
            if detour:
                @pl.when(via_source(side))
                def _(side=side, s=s, heads=heads):
                    via_v_in(side, heads, s).start()

                @pl.when(sideways[side][0] & ~via_source(side))
                def _(side=side, s=s, heads=heads):
                    v_copy(side, heads, s).start()
            else:
                @pl.when(sideways[side][0])
                def _(side=side, s=s, heads=heads):
                    v_copy(side, heads, s).start()

    @pl.when(sec == sections - 1)
    def _():
        handed[...] = jnp.zeros_like(handed)

    @pl.when(sec < sections - 1)
    def _():
        sec_copy.wait_recv()

    loads[4].wait()

    @pl.loop(0, HEADS)
    def _(h):
        at = head_cols(h)
        gb[h, pl.ds(128, 128)] = (c_ref[:, at].astype(f32) + handed[:, at].astype(f32)).astype(bf16)

    for d in range(2):
        @pl.when(vertical[d][1])
        def _(d=d):
            bias_copy(d).wait_recv()

    nt = (((1,), (1,)), ((), ()))
    nn = (((1,), (0,)), ((), ()))
    tn = (((0,), (0,)), ((), ()))

    def dot(a, b, dims):
        return lax.dot_general(a, b, dims, preferred_element_type=f32)

    slots = [slice(n * 128, n * 128 + 128) for n in range(3)]

    @pl.loop(0, groups)
    def _(g):
        for d in range(2):
            @pl.when(vertical[d][1])
            def _(d=d):
                q_copy(d, g).wait_recv()

        @pl.when(lax.rem(g, per_span) == 0)
        def _():
            s = lax.div(g, per_span)
            heads = pl.ds(s * SPAN, SPAN)
            for side in range(2):
                @pl.when(sideways[side][1])
                def _(side=side):
                    k_copy(side, heads, s).wait_recv()

        for i in range(GROUP):
            h = g * GROUP + i
            part = dot(kb[h], qb[h], nt)
            for n, at in enumerate(slots):
                rows = part[:, at] * scale
                scores = jnp.concatenate(
                    [
                        (rows[:128].reshape(8, 2, 8, LANES) + bias[n, 0:2][None]).reshape(128, LANES),
                        (rows[128:192].reshape(8, 8, LANES) + bias[n, 2][None]).reshape(64, LANES),
                        (rows[192:].reshape(8, 8, LANES) + bias[n, 3][None]).reshape(64, LANES),
                    ],
                    axis=0,
                )
                top = jnp.max(scores, axis=0, keepdims=True)
                exps = jnp.exp2(scores - top)
                weights[h, :, at] = exps
                xs1[g, n, pl.ds(i, 1)] = top
                xs1[g, n, pl.ds(GROUP + i, 1)] = jnp.sum(exps, axis=0, keepdims=True)

        stat_start(xs1, xr1, send_x1, recv_x1, g)

        @pl.when(g < groups - AHEAD)
        def _():
            issue(q_copy, g + AHEAD)

        @pl.when(g >= groups - AHEAD)
        def _():
            issue(g_copy, g + AHEAD - groups)

        if detour:
            @pl.when(lax.rem(g, per_span) == per_span - 1)
            def _():
                s = lax.div(g, per_span)
                heads = pl.ds(s * SPAN, SPAN)
                for side in range(2):
                    @pl.when(via_holder(side))
                    def _(side=side):
                        via_v_in(side, heads, s).wait_recv()
                        via_v_out(side, heads, s).start()

    others = ((0, 4), (1, 2), (3, 5))

    def probabilities(g):
        @pl.when(lax.rem(g, per_span) == 0)
        def _():
            s = lax.div(g, per_span)
            heads = pl.ds(s * SPAN, SPAN)
            for side in range(2):
                @pl.when(sideways[side][1])
                def _(side=side):
                    v_copy(side, heads, s).wait_recv()

        stat_wait(xs1, xr1, send_x1, recv_x1, g)
        for d in range(2):
            @pl.when(vertical[d][1])
            def _(d=d):
                g_copy(d, g).wait_recv()

        factors = []
        for n in range(3):
            stats = [xs1[g, n], xr1[g, others[n][0]], xr1[g, others[n][1]]]
            tops = [stat[:GROUP] for stat in stats]
            top = jnp.maximum(jnp.maximum(tops[0], tops[1]), tops[2])
            shifts = [jnp.exp2(t - top) for t in tops]
            total = sum(s * stat[GROUP:2 * GROUP] for s, stat in zip(shifts, stats))
            factors.append(shifts[0] * (1.0 / total))
        for i in range(GROUP):
            h = g * GROUP + i
            part = dot(vb[h], gb[h], nt)
            lows = []
            for n, at in enumerate(slots):
                probs = weights[h, :, at] * factors[n][i:i + 1]
                low = probs.astype(bf16)
                weights[h, :, at] = probs
                grads[h, :, at] = part[:, at]
                xs2[g, n, pl.ds(i, 1)] = jnp.sum(low.astype(f32) * part[:, at], axis=0, keepdims=True)
                lows.append(low)
            grad_value = dot(jnp.concatenate(lows, axis=1), gb[h], nn)
            dv_own[h] = grad_value[:128]
            dv_send[0, h] = grad_value[128:192].astype(bf16)
            dv_send[1, h] = grad_value[192:].astype(bf16)

        stat_start(xs2, xr2, send_x2, recv_x2, g)

        @pl.when(g < groups - AHEAD)
        def _():
            issue(g_copy, g + AHEAD)

        heads = pl.ds(g * GROUP, GROUP)
        s = lax.div(g, per_span)
        for side in range(2):
            if detour:
                @pl.when(via_source(side))
                def _(side=side):
                    via_dv_in(side, heads, g).start()

                @pl.when(sideways[side][0] & ~via_source(side))
                def _(side=side):
                    dv_copy(side, heads, s).start()
            else:
                @pl.when(sideways[side][0])
                def _(side=side):
                    dv_copy(side, heads, s).start()

    def gradients(g):
        stat_wait(xs2, xr2, send_x2, recv_x2, g)
        deltas = [
            xs2[g, n, pl.ds(0, GROUP)]
            + xr2[g, others[n][0], pl.ds(0, GROUP)]
            + xr2[g, others[n][1], pl.ds(0, GROUP)]
            for n in range(3)
        ]
        for i in range(GROUP):
            h = g * GROUP + i
            scores = jnp.concatenate(
                [
                    (
                        weights[h, :, at] * (grads[h, :, at] - deltas[n][i:i + 1]) * inv_root
                    ).astype(bf16)
                    for n, at in enumerate(slots)
                ],
                axis=1,
            )
            grad_query = dot(scores, kb[h], tn)
            dq_send[0, h] = grad_query[:128].astype(bf16)
            dq_own[h] = grad_query[128:256]
            dq_send[1, h] = grad_query[256:].astype(bf16)
            grad_key = dot(scores, qb[h], nn)
            dk_own[h] = grad_key[:128]
            dk_send[0, h] = grad_key[128:192].astype(bf16)
            dk_send[1, h] = grad_key[192:].astype(bf16)

        heads = pl.ds(g * GROUP, GROUP)
        s = lax.div(g, per_span)
        for d in range(2):
            @pl.when(vertical[d][0])
            def _(d=d):
                dq_copy(d, g, heads).start()

        for side in range(2):
            @pl.when(sideways[side][0])
            def _(side=side):
                dk_copy(side, heads, s).start()

            if detour:
                @pl.when(via_holder(side))
                def _(side=side):
                    via_dv_in(side, heads, g).wait_recv()
                    via_dv_out(side, heads, s).start()

    @pl.loop(0, groups + LAG)
    def _(t):
        @pl.when(t < groups)
        def _():
            probabilities(t)

        @pl.when(t >= LAG)
        def _():
            gradients(t - LAG)

    def fold(own, recv, h):
        blocks = own[h].reshape(8, 2, 8, LANES)
        sides = [recv[side, h].astype(f32).reshape(8, 1, 8, LANES) for side in range(2)]
        return (blocks + jnp.concatenate(sides, axis=1)).reshape(128, LANES).astype(bf16)

    @pl.loop(0, spans)
    def _(s):
        heads = pl.ds(s * SPAN, SPAN)
        for side in range(2):
            @pl.when(sideways[1 - side][1])
            def _(side=side):
                dv_copy(1 - side, heads, s).wait_recv()
                dk_copy(1 - side, heads, s).wait_recv()

        for i in range(SPAN):
            h = s * SPAN + i
            ov_ref[:, head_cols(h)] = fold(dv_own, dv_recv, h)
            ok_ref[:, head_cols(h)] = fold(dk_own, dk_recv, h)

    @pl.loop(0, groups)
    def _(g):
        heads = pl.ds(g * GROUP, GROUP)
        for d in range(2):
            @pl.when(vertical[1 - d][1])
            def _(d=d):
                dq_copy(1 - d, g, heads).wait_recv()

        for i in range(GROUP):
            h = g * GROUP + i
            oq_ref[:, head_cols(h)] = (
                dq_own[h] + dq_recv[0, h].astype(f32) + dq_recv[1, h].astype(f32)
            ).astype(bf16)

    @pl.when(sec > 0)
    def _():
        sec_copy.wait_send()

    every = pl.ds(0, HEADS)
    for d in range(2):
        @pl.when(vertical[d][0])
        def _(d=d):
            bias_copy(d).wait_send()
            rows_copy(qb, send_q, recv_q, d, every, 0).wait_send()
            rows_copy(gb, send_g, recv_g, d, every, 0).wait_send()
            dq_copy(d, 0, every).wait_send()

    for m in range(4):
        @pl.when(stat_moves[m][0])
        def _(m=m):
            stat_copy(xs1, xr1, send_x1, recv_x1, m, pl.ds(0, groups)).wait_send()
            stat_copy(xs2, xr2, send_x2, recv_x2, m, pl.ds(0, groups)).wait_send()

    for side in range(2):
        @pl.when(sideways[side][0])
        def _(side=side):
            k_copy(side, every, 0).wait_send()
            v_copy(side, every, 0).wait_send()
            dk_copy(side, every, 0).wait_send()
            dv_copy(side, every, 0).wait_send()

        if detour:
            @pl.when(via_holder(side))
            def _(side=side):
                via_v_out(side, every, 0).wait_send()
                via_dv_out(side, every, 0).wait_send()


def store_kernel(aq, ak, av, oq, ok, ov, sems):
    stores = [
        pltpu.make_async_copy(src, dst, sems.at[n])
        for n, (src, dst) in enumerate(((aq, oq), (ak, ok), (av, ov)))
    ]
    for store in stores:
        store.start()
    for store in stores:
        store.wait()


def relay_body(queries, keys, values, cotangent, upstream, block_mask):
    sections, rows_n, cols_n = (lax.axis_size(a) for a in ("section", "ha", "wa"))
    shape = queries.shape
    tokens = shape[1] * shape[2] * shape[3]
    flat = (tokens, shape[4])
    groups, spans = HEADS // GROUP, HEADS // SPAN
    bf16, f32 = jnp.bfloat16, jnp.float32
    dma = pltpu.SemaphoreType.DMA
    vmem = pltpu.VMEM
    out = pl.pallas_call(
        functools.partial(relay_kernel, sections, rows_n, cols_n),
        out_shape=[vmem(flat, bf16)] * 3,
        in_specs=[pl.BlockSpec(memory_space=pltpu.HBM)] * 6,
        out_specs=[pl.BlockSpec(memory_space=pltpu.VMEM)] * 3,
        scratch_shapes=[
            vmem(flat, bf16), vmem(flat, bf16), vmem(flat, bf16), vmem(flat, bf16),
            pltpu.SMEM((2, 9), jnp.int32),
            vmem(flat, bf16),
            vmem((HEADS, 384, LANES), bf16), vmem((HEADS, 384, LANES), bf16),
            vmem((HEADS, 256, LANES), bf16), vmem((HEADS, 256, LANES), bf16),
            vmem((2, HEADS, 64, LANES), bf16), vmem((2, HEADS, 64, LANES), bf16),
            vmem((3, 4, 8, LANES), f32), vmem((3, 4, 8, LANES), f32),
            vmem((HEADS, 256, 384), f32), vmem((HEADS, 256, 384), f32),
            vmem((groups, 3, 8, LANES), f32), vmem((groups, 6, 8, LANES), f32),
            vmem((groups, 3, 8, LANES), f32), vmem((groups, 6, 8, LANES), f32),
            vmem((HEADS, 128, LANES), f32),
            vmem((2, HEADS, 128, LANES), bf16), vmem((2, HEADS, 128, LANES), bf16),
            vmem((HEADS, 128, LANES), f32), vmem((HEADS, 128, LANES), f32),
            vmem((2, HEADS, 64, LANES), bf16), vmem((2, HEADS, 64, LANES), bf16),
            vmem((2, HEADS, 64, LANES), bf16), vmem((2, HEADS, 64, LANES), bf16),
            vmem((HEADS, 64, LANES), bf16), vmem((HEADS, 64, LANES), bf16),
            dma((5,)), dma((2,)), dma((2, 2)),
            dma((2,)), dma((2,)), dma((2,)), dma((2,)), dma((2,)), dma((2,)), dma((2,)),
            dma((4,)), dma((4,)), dma((2,)),
            dma((2, groups)), dma((2, groups)), dma((2, groups)),
            dma((2, spans)), dma((2, spans)), dma((2, spans)), dma((2, spans)),
            dma((4, groups)), dma((4, groups)), dma((spans,)), dma((groups,)),
        ],
        compiler_params=pltpu.CompilerParams(
            collective_id=0, has_side_effects=True, vmem_limit_bytes=40 * 2**20
        ),
    )(
        queries.reshape(flat), keys.reshape(flat), values.reshape(flat),
        cotangent.reshape(flat), upstream.reshape(flat), block_mask.reshape(2, 9),
    )
    out = pl.pallas_call(
        store_kernel,
        out_shape=[jax.ShapeDtypeStruct(flat, bf16)] * 3,
        in_specs=[pl.BlockSpec(memory_space=pltpu.VMEM)] * 3,
        out_specs=[pl.BlockSpec(memory_space=pltpu.HBM)] * 3,
        scratch_shapes=[dma((3,))],
        compiler_params=pltpu.CompilerParams(vmem_limit_bytes=4 * 2**20),
    )(*out)
    return tuple(x.reshape(shape) for x in out)


def solution(mesh):
    return jax.shard_map(
        relay_body,
        mesh=mesh,
        in_specs=(
            P("section", None, "ha", "wa", None),
            P("section", None, "ha", "wa", None),
            P("section", None, "ha", "wa", None),
            P("section", None, "ha", "wa", None),
            P("section", None, "ha", "wa", None),
            P("section", "ha", "wa", None),
        ),
        out_specs=(
            P("section", None, "ha", "wa", None),
            P("section", None, "ha", "wa", None),
            P("section", None, "ha", "wa", None),
        ),
        check_vma=False,
    )
```

```python
import functools

import jax
import jax.numpy as jnp
from jax import lax
from jax.experimental import pallas as pl
from jax.experimental.pallas import tpu as pltpu
from jax.sharding import PartitionSpec as P

HEADS = 12
HEAD_DIM = 128
TILE = 8


NEG = -1e30
LANES = 128
GROUP = 2
SPAN = 4
FIRST = (0, 1)
SECOND = (6, 2, 7)
STEPS = (
    (0, 0, 8, 3), (0, 1, 9, 4), (0, 2, 10, 5), (1, 0, 11, -1), (0, 3, 12, -1), (1, 1, -1, -1),
    (0, 4, 13, -1), (1, 2, -1, -1), (0, 5, 14, -1), (1, 3, 15, -1), (1, 4, 16, -1), (1, 5, 17, -1),
)
MESH_ID = pl.DeviceIdType.MESH


def relay_kernel(
    sections, rows_n, cols_n,
    q_hbm, k_hbm, v_hbm, c_hbm, u_hbm, mask_hbm,
    oq_ref, ok_ref, ov_ref,
    q_ref, k_ref, v_ref, c_ref, mask_ref, handed,
    qb, gb, kb, vb, k_send, v_send, bias_send, bias, bias_tiles,
    weights, grads, tops, xs1, xr1,
    dq_own, dq_send, dq_recv, dk_own, dv_own, dk_send, dv_send, dk_recv, dv_recv, via_v, via_dv,
    load_sem, sec_sem, bias_sem, send_q, send_g, send_dq, send_k, send_v, send_dk, send_dv,
    send_x1, send_via, recv_q, recv_g, recv_dq, recv_k, recv_v, recv_dk, recv_dv,
    recv_x1, recv_via_v, recv_via_dv,
):
    f32, bf16 = jnp.float32, jnp.bfloat16
    sec = lax.axis_index("section")
    row = lax.axis_index("ha")
    col = lax.axis_index("wa")
    groups = HEADS // GROUP
    spans = HEADS // SPAN
    per_span = SPAN // GROUP
    inv_root = HEAD_DIM ** (-0.5)
    scale = inv_root * 1.4426950408889634
    has_up, has_down = row > 0, row < rows_n - 1
    has_up2, has_down2 = row > 1, row < rows_n - 2
    has_left, has_right = col > 0, col < cols_n - 1
    detour = cols_n == 4

    loads = [
        pltpu.make_async_copy(src, dst, load_sem.at[n])
        for n, (src, dst) in enumerate(
            ((q_hbm, q_ref), (k_hbm, k_ref), (v_hbm, v_ref), (mask_hbm, mask_ref), (c_hbm, c_ref))
        )
    ]
    for load in loads:
        load.start()

    barrier = pltpu.get_barrier_semaphore()
    greeted = [
        (has_up, {"ha": row - 1}),
        (has_down, {"ha": row + 1}),
        (has_up2, {"ha": row - 2}),
        (has_down2, {"ha": row + 2}),
        (has_left, {"wa": col - 1}),
        (has_right, {"wa": col + 1}),
        (sec > 0, {"section": sec - 1}),
        (sec < sections - 1, {"section": sec + 1}),
    ]
    if detour:
        greeted.append((col >= 0, {"wa": lax.rem(col + 2, 4)}))
    expected = jnp.int32(0)
    for cond, dev in greeted:
        @pl.when(cond)
        def _(dev=dev):
            pl.semaphore_signal(barrier, inc=1, device_id=dev, device_id_type=MESH_ID)

        expected = expected + cond.astype(jnp.int32)

    def remote(src, dst, send, recv, dev):
        return pltpu.make_async_remote_copy(
            src_ref=src, dst_ref=dst, send_sem=send, recv_sem=recv,
            device_id=dev, device_id_type=MESH_ID,
        )

    vertical = ((has_up, has_down, {"ha": row - 1}), (has_down, has_up, {"ha": row + 1}))
    sideways = ((has_left, has_right, {"wa": col - 1}), (has_right, has_left, {"wa": col + 1}))

    def slot_rows(d):
        return pl.ds(256 - 256 * d, 128)

    def halo_rows(side):
        return pl.ds(192 - 64 * side, 64)

    sec_copy = remote(u_hbm, handed, sec_sem.at[0], sec_sem.at[1], {"section": sec - 1})

    def bias_copy(d):
        return remote(
            bias_send.at[2 * d], bias.at[2 - 2 * d], bias_sem.at[0], bias_sem.at[1],
            vertical[d][2],
        )

    def rows_copy(buf, send, recv, d, heads, g):
        return remote(
            buf.at[heads, pl.ds(128, 128)], buf.at[heads, slot_rows(d)],
            send.at[0], recv.at[g], vertical[d][2],
        )

    def q_copy(d, g):
        return rows_copy(qb, send_q, recv_q, d, pl.ds(g * GROUP, GROUP), g)

    def g_copy(d, g):
        return rows_copy(gb, send_g, recv_g, d, pl.ds(g * GROUP, GROUP), g)

    def dq_copy(d, g):
        heads = pl.ds(g * GROUP, GROUP)
        return remote(
            dq_send.at[d, heads], dq_recv.at[1 - d, heads],
            send_dq.at[0], recv_dq.at[g], vertical[d][2],
        )

    def k_copy(side, heads, s):
        return remote(
            k_send.at[side, heads], kb.at[heads, halo_rows(side)],
            send_k.at[0], recv_k.at[s], sideways[side][2],
        )

    def v_copy(side, heads, s):
        return remote(
            v_send.at[side, heads], vb.at[heads, halo_rows(side)],
            send_v.at[0], recv_v.at[s], sideways[side][2],
        )

    def dk_copy(side, heads, s):
        return remote(
            dk_send.at[side, heads], dk_recv.at[1 - side, heads],
            send_dk.at[0], recv_dk.at[s], sideways[side][2],
        )

    def dv_copy(side, heads, s):
        return remote(
            dv_send.at[side, heads], dv_recv.at[1 - side, heads],
            send_dv.at[0], recv_dv.at[s], sideways[side][2],
        )

    def via_source(side):
        return col == (2, 1)[side]

    def via_holder(side):
        return col == (0, 3)[side]

    def via_v_in(side, heads, s):
        return remote(
            v_send.at[side, heads], via_v.at[heads], send_v.at[0], recv_via_v.at[s],
            {"wa": jnp.int32((0, 3)[side])},
        )

    def via_v_out(side, heads, s):
        return remote(
            via_v.at[heads], vb.at[heads, halo_rows(side)], send_via.at[0], recv_v.at[s],
            {"wa": jnp.int32((1, 2)[side])},
        )

    def via_dv_in(side, heads, g):
        return remote(
            dv_send.at[side, heads], via_dv.at[heads], send_dv.at[0], recv_via_dv.at[g],
            {"wa": jnp.int32((0, 3)[side])},
        )

    def via_dv_out(side, heads, s):
        return remote(
            via_dv.at[heads], dv_recv.at[1 - side, heads], send_via.at[1],
            recv_dv.at[s], {"wa": jnp.int32((1, 2)[side])},
        )

    stat_moves = (
        (has_up, has_down, {"ha": row - 1}, pl.ds(0, 2), pl.ds(2, 2)),
        (has_down, has_up, {"ha": row + 1}, pl.ds(1, 2), pl.ds(0, 2)),
        (has_up2, has_down2, {"ha": row - 2}, pl.ds(0, 1), pl.ds(5, 1)),
        (has_down2, has_up2, {"ha": row + 2}, pl.ds(2, 1), pl.ds(4, 1)),
    )

    def stat_copy(xs, xr, send, recv, m, g):
        _, _, dev, mine, theirs = stat_moves[m]
        return remote(xs.at[g, mine], xr.at[g, theirs], send.at[0], recv.at[g], dev)

    def stat_start(xs, xr, send, recv, g):
        for m in range(4):
            @pl.when(stat_moves[m][0])
            def _(m=m):
                stat_copy(xs, xr, send, recv, m, g).start()

    def stat_tiles(at):
        return 2 * ((at > 0) + (at < rows_n - 1)) + (at > 1) + (at < rows_n - 2)

    tiles_here = sum(
        n * cond.astype(jnp.int32)
        for n, cond in ((2, has_up), (2, has_down), (1, has_up2), (1, has_down2))
    )

    def stat_wait(xr, sem, g):
        for tiles in sorted({stat_tiles(at) for at in range(rows_n)} - {0}):
            @pl.when(tiles_here == tiles)
            def _(tiles=tiles):
                ref = xr.at[g, pl.ds(0, tiles)]
                pltpu.make_async_copy(ref, ref, sem).wait()

    def wait_pair(first, second, ref_both, ref_one, sem):
        @pl.when(first & second)
        def _():
            pltpu.make_async_copy(ref_both, ref_both, sem).wait()

        @pl.when(first ^ second)
        def _():
            pltpu.make_async_copy(ref_one, ref_one, sem).wait()

    def wait_rows(buf, sem, heads):
        wait_pair(
            has_up, has_down, buf.at[heads, pl.ds(0, 256)], buf.at[heads, pl.ds(0, 128)], sem
        )

    def wait_halos(buf, sem, heads):
        wait_pair(
            has_left, has_right, buf.at[heads, pl.ds(128, 128)], buf.at[heads, pl.ds(128, 64)], sem
        )

    def wait_two(buf, sem, heads, first, second):
        wait_pair(first, second, buf.at[:, heads], buf.at[0, heads], sem)

    def issue(chunk):
        kind, g = lax.div(chunk, groups), lax.rem(chunk, groups)
        for d in range(2):
            for n, copy in enumerate((q_copy, g_copy, dq_copy)):
                @pl.when(vertical[d][0] & (chunk >= 0) & (kind == n))
                def _(d=d, copy=copy):
                    copy(d, g).start()

    def head_cols(head):
        return pl.ds(pl.multiple_of(head * LANES, LANES), LANES)

    def split(block):
        tiles = block.astype(f32).reshape(8, 2, 8, LANES)
        return [tiles[:, t].reshape(64, LANES).astype(bf16) for t in range(2)]

    def spread(ref, buf, send):
        @pl.loop(0, HEADS)
        def _(h):
            block = ref[:, head_cols(h)]
            buf[h, pl.ds(0, 128)] = block
            for side, part in enumerate(split(block)):
                send[side, h] = part

    loads[0].wait()

    @pl.loop(0, HEADS)
    def _(h):
        qb[h, pl.ds(128, 128)] = q_ref[:, head_cols(h)]

    loads[1].wait()
    spread(k_ref, kb, k_send)

    loads[3].wait()
    lane = lax.broadcasted_iota(jnp.int32, (1, LANES), 1)
    first_tile = lax.rem(lane // TILE, 2) == 0
    dead = jnp.int32(0)
    left = jnp.where(has_left, 1, 0)
    right = jnp.where(has_right, 1, 0)
    for i in range(3):
        entry = [[mask_ref[t, 3 * i + j] for j in range(3)] for t in range(2)]
        for n, (first, second) in enumerate((
            (entry[0][1], entry[1][0]),
            (entry[0][2], entry[1][1]),
            (entry[0][0] * left, dead),
            (dead, entry[1][2] * right),
        )):
            seen = jnp.where(first_tile, first, second)
            bias_send[i, pl.ds(n, 1)] = jnp.where(seen > 0, 0.0, NEG).astype(f32)
    bias[1] = bias_send[1]

    pl.semaphore_wait(barrier, expected)

    issue(jnp.int32(FIRST[0]))
    for d in range(2):
        @pl.when(vertical[d][0])
        def _(d=d):
            bias_copy(d).start()

    @pl.when(sec > 0)
    def _():
        sec_copy.start()

    for chunk in FIRST[1:]:
        issue(jnp.int32(chunk))

    def start_k(g):
        for side in range(2):
            @pl.when(sideways[side][0])
            def _(side=side):
                k_copy(side, pl.ds(g * GROUP, GROUP), g).start()

    def start_v(g):
        heads = pl.ds(g * GROUP, GROUP)
        for side in range(2):
            if detour:
                @pl.when(via_source(side))
                def _(side=side):
                    via_v_in(side, heads, g).start()

            @pl.when(sideways[side][0] & ~via_source(side) if detour else sideways[side][0])
            def _(side=side):
                v_copy(side, heads, g).start()

    def start_kv(g):
        start_k(g)
        start_v(g)

    def forward_v(g):
        for side in range(2):
            @pl.when(via_holder(side))
            def _(side=side):
                heads = pl.ds(g * GROUP, GROUP)
                via_v_in(side, heads, g).wait_recv()
                via_v_out(side, heads, g).start()

    def forward_dv(g):
        for side in range(2):
            @pl.when(via_holder(side))
            def _(side=side):
                heads = pl.ds(g * GROUP, GROUP)
                via_dv_in(side, heads, g).wait_recv()
                via_dv_out(side, heads, lax.div(g, per_span)).start()

    start_k(0)
    start_k(1)
    loads[2].wait()
    spread(v_ref, vb, v_send)
    start_v(0)
    start_v(1)

    for cond, at in ((row == 0, 0), (row == rows_n - 1, 256)):
        @pl.when(cond)
        def _(at=at):
            bias[2 * at // 256] = jnp.zeros((4, LANES), f32)

            @pl.loop(0, HEADS)
            def _(h):
                qb[h, pl.ds(at, 128)] = jnp.zeros((128, LANES), bf16)
                gb[h, pl.ds(at, 128)] = jnp.zeros((128, LANES), bf16)
                dq_recv[at // 256, h] = jnp.zeros((128, LANES), bf16)

    for cond, side in ((col == 0, 0), (col == cols_n - 1, 1)):
        @pl.when(cond)
        def _(side=side):
            @pl.loop(0, HEADS)
            def _(h):
                kb[h, pl.ds(128 + 64 * side, 64)] = jnp.zeros((64, LANES), bf16)
                vb[h, pl.ds(128 + 64 * side, 64)] = jnp.zeros((64, LANES), bf16)
                dk_recv[side, h] = jnp.zeros((64, LANES), bf16)
                dv_recv[side, h] = jnp.zeros((64, LANES), bf16)

    stat_row = lax.broadcasted_iota(jnp.int32, (2 * GROUP, LANES), 0)
    no_stat = jnp.where(stat_row < GROUP, NEG, 0.0).astype(f32)
    for cond, pieces in (
        (row == 0, (0, 1)), (row < 2, (4,)),
        (row == rows_n - 1, (2, 3)), (row > rows_n - 3, (5,)),
    ):
        @pl.when(cond)
        def _(pieces=pieces):
            for g in range(groups):
                for piece in pieces:
                    xr1[g, piece] = no_stat

    @pl.when(sec == sections - 1)
    def _():
        handed[...] = jnp.zeros_like(handed)

    @pl.when(sec < sections - 1)
    def _():
        sec_copy.wait_recv()

    loads[4].wait()

    @pl.loop(0, HEADS)
    def _(h):
        at = head_cols(h)
        gb[h, pl.ds(128, 128)] = (c_ref[:, at].astype(f32) + handed[:, at].astype(f32)).astype(bf16)

    for chunk in SECOND:
        issue(jnp.int32(chunk))

    for g in range(2):
        if detour:
            forward_v(g)
        start_kv(g + 2)

    wait_pair(has_up, has_down, bias.at[pl.ds(0, 2)], bias.at[0], bias_sem.at[1])
    for n in range(3):
        for k in range(4):
            bias_tiles[n, k] = jnp.broadcast_to(bias[n, pl.ds(k, 1)], (8, LANES))

    nt = (((1,), (1,)), ((), ()))
    nn = (((1,), (0,)), ((), ()))
    tn = (((0,), (0,)), ((), ()))

    def dot(a, b, dims):
        return lax.dot_general(a, b, dims, preferred_element_type=f32)

    slots = [slice(n * 128, n * 128 + 128) for n in range(3)]

    def exponents(g):
        heads = pl.ds(g * GROUP, GROUP)
        wait_rows(qb, recv_q.at[g], heads)
        wait_halos(kb, recv_k.at[g], heads)
        wait_rows(gb, recv_g.at[g], heads)
        wait_halos(vb, recv_v.at[g], heads)
        for i in range(GROUP):
            h = g * GROUP + i
            part = dot(kb[h], qb[h], nt)
            grad_part = dot(vb[h], gb[h], nt)
            for n, at in enumerate(slots):
                rows = part[:, at] * scale
                scores = jnp.concatenate(
                    [
                        (rows[:128].reshape(8, 2, 8, LANES) + bias_tiles[n, 0:2][None]).reshape(128, LANES),
                        (rows[128:192].reshape(8, 8, LANES) + bias_tiles[n, 2][None]).reshape(64, LANES),
                        (rows[192:].reshape(8, 8, LANES) + bias_tiles[n, 3][None]).reshape(64, LANES),
                    ],
                    axis=0,
                )
                top = jnp.max(scores, axis=0, keepdims=True)
                exps = jnp.exp2(scores - top)
                weights[h, :, at] = exps
                grads[h, :, at] = grad_part[:, at]
                total = jnp.sum(exps, axis=0, keepdims=True)
                delta = jnp.sum(exps * grad_part[:, at], axis=0, keepdims=True)
                tops[g, n, pl.ds(i, 1)] = top
                xs1[g, n, pl.ds(i, 1)] = top + jnp.log(total) * 1.4426950408889634
                xs1[g, n, pl.ds(GROUP + i, 1)] = delta / total

        stat_start(xs1, xr1, send_x1, recv_x1, g)

        @pl.when(g + 2 < groups)
        def _():
            if detour:
                forward_v(g + 2)

            @pl.when(g + 4 < groups)
            def _():
                start_kv(g + 4)

    others = ((0, 4), (1, 2), (3, 5))

    def gradients(g):
        stat_wait(xr1, recv_x1.at[g], g)
        factors, deltas = [], []
        for n in range(3):
            stats = [xs1[g, n], xr1[g, others[n][0]], xr1[g, others[n][1]]]
            top = jnp.maximum(
                jnp.maximum(stats[0][:GROUP], stats[1][:GROUP]), stats[2][:GROUP]
            )
            shares = [jnp.exp2(stat[:GROUP] - top) for stat in stats]
            inverse = 1.0 / (shares[0] + shares[1] + shares[2])
            delta = sum(share * stat[GROUP:] for share, stat in zip(shares, stats))
            factors.append(jnp.exp2(tops[g, n, pl.ds(0, GROUP)] - top) * inverse)
            deltas.append(delta * inverse)
        for i in range(GROUP):
            h = g * GROUP + i
            lows, scores = [], []
            for n, at in enumerate(slots):
                probs = weights[h, :, at] * factors[n][i:i + 1]
                lows.append(probs.astype(bf16))
                scores.append((probs * (grads[h, :, at] - deltas[n][i:i + 1]) * inv_root).astype(bf16))
            low = jnp.concatenate(lows, axis=1)
            score = jnp.concatenate(scores, axis=1)
            grad_query = dot(score, kb[h], tn)
            dq_send[0, h] = grad_query[:128].astype(bf16)
            dq_own[h] = grad_query[128:256]
            dq_send[1, h] = grad_query[256:].astype(bf16)
            grad_key = dot(score, qb[h], nn)
            dk_own[h] = grad_key[:128]
            dk_send[0, h] = grad_key[128:192].astype(bf16)
            dk_send[1, h] = grad_key[192:].astype(bf16)
            grad_value = dot(low, gb[h], nn)
            dv_own[h] = grad_value[:128]
            dv_send[0, h] = grad_value[128:192].astype(bf16)
            dv_send[1, h] = grad_value[192:].astype(bf16)

        heads = pl.ds(g * GROUP, GROUP)
        s = lax.div(g, per_span)
        for side in range(2):
            around = via_source(side) & (g < groups - 1) if detour else None
            if detour:
                @pl.when(around)
                def _(side=side):
                    via_dv_in(side, heads, g).start()

            @pl.when(sideways[side][0] & ~around if detour else sideways[side][0])
            def _(side=side):
                dv_copy(side, heads, s).start()

            @pl.when(sideways[side][0])
            def _(side=side):
                dk_copy(side, heads, s).start()

        if detour:
            @pl.when(g > 0)
            def _():
                forward_dv(g - 1)

    @pl.loop(0, len(STEPS))
    def _(t):
        stage, g, first, second = (
            sum((t == n).astype(jnp.int32) * step[at] for n, step in enumerate(STEPS))
            for at in range(4)
        )
        for n, run in enumerate((exponents, gradients)):
            @pl.when(stage == n)
            def _(run=run):
                run(g)

        issue(first)
        issue(second)

    def fold(own, recv, h):
        blocks = own[h].reshape(8, 2, 8, LANES)
        sides = [recv[side, h].astype(f32).reshape(8, 1, 8, LANES) for side in range(2)]
        return (blocks + jnp.concatenate(sides, axis=1)).reshape(128, LANES).astype(bf16)

    @pl.loop(0, spans)
    def _(s):
        heads = pl.ds(s * SPAN, SPAN)
        wait_two(dv_recv, recv_dv.at[s], heads, has_left, has_right)
        wait_two(dk_recv, recv_dk.at[s], heads, has_left, has_right)
        for i in range(SPAN):
            h = s * SPAN + i
            ov_ref[:, head_cols(h)] = fold(dv_own, dv_recv, h)
            ok_ref[:, head_cols(h)] = fold(dk_own, dk_recv, h)

    @pl.loop(0, groups)
    def _(g):
        heads = pl.ds(g * GROUP, GROUP)
        wait_two(dq_recv, recv_dq.at[g], heads, has_up, has_down)
        for i in range(GROUP):
            h = g * GROUP + i
            oq_ref[:, head_cols(h)] = (
                dq_own[h] + dq_recv[0, h].astype(f32) + dq_recv[1, h].astype(f32)
            ).astype(bf16)

    @pl.when(sec > 0)
    def _():
        sec_copy.wait_send()

    every = pl.ds(0, HEADS)
    wait_pair(has_up, has_down, bias.at[pl.ds(0, 2)], bias.at[0], bias_sem.at[0])
    wait_rows(qb, send_q.at[0], every)
    wait_rows(gb, send_g.at[0], every)
    wait_two(dq_send, send_dq.at[0], every, has_up, has_down)
    stat_wait(xr1, send_x1.at[0], pl.ds(0, groups))
    for buf, sem in ((k_send, send_k), (v_send, send_v), (dk_send, send_dk), (dv_send, send_dv)):
        wait_two(buf, sem.at[0], every, has_left, has_right)
    if detour:
        for side in range(2):
            @pl.when(via_holder(side))
            def _(side=side):
                via_v_out(side, every, 0).wait_send()
                via_dv_out(side, pl.ds(0, HEADS - GROUP), 0).wait_send()


def store_kernel(aq, ak, av, oq, ok, ov, sems):
    stores = [
        pltpu.make_async_copy(src, dst, sems.at[n])
        for n, (src, dst) in enumerate(((aq, oq), (ak, ok), (av, ov)))
    ]
    for store in stores:
        store.start()
    for store in stores:
        store.wait()


def relay_body(queries, keys, values, cotangent, upstream, block_mask):
    sections, rows_n, cols_n = (lax.axis_size(a) for a in ("section", "ha", "wa"))
    shape = queries.shape
    tokens = shape[1] * shape[2] * shape[3]
    flat = (tokens, shape[4])
    groups, spans = HEADS // GROUP, HEADS // SPAN
    bf16, f32 = jnp.bfloat16, jnp.float32
    dma = pltpu.SemaphoreType.DMA
    vmem = pltpu.VMEM
    out = pl.pallas_call(
        functools.partial(relay_kernel, sections, rows_n, cols_n),
        out_shape=[vmem(flat, bf16)] * 3,
        in_specs=[pl.BlockSpec(memory_space=pltpu.HBM)] * 6,
        out_specs=[pl.BlockSpec(memory_space=pltpu.VMEM)] * 3,
        scratch_shapes=[
            vmem(flat, bf16), vmem(flat, bf16), vmem(flat, bf16), vmem(flat, bf16),
            pltpu.SMEM((2, 9), jnp.int32),
            vmem(flat, bf16),
            vmem((HEADS, 384, LANES), bf16), vmem((HEADS, 384, LANES), bf16),
            vmem((HEADS, 256, LANES), bf16), vmem((HEADS, 256, LANES), bf16),
            vmem((2, HEADS, 64, LANES), bf16), vmem((2, HEADS, 64, LANES), bf16),
            vmem((3, 4, LANES), f32), vmem((3, 4, LANES), f32), vmem((3, 4, 8, LANES), f32),
            vmem((HEADS, 256, 384), f32), vmem((HEADS, 256, 384), f32),
            vmem((groups, 3, 8, LANES), f32),
            vmem((groups, 3, 2 * GROUP, LANES), f32), vmem((groups, 6, 2 * GROUP, LANES), f32),
            vmem((HEADS, 128, LANES), f32),
            vmem((2, HEADS, 128, LANES), bf16), vmem((2, HEADS, 128, LANES), bf16),
            vmem((HEADS, 128, LANES), f32), vmem((HEADS, 128, LANES), f32),
            vmem((2, HEADS, 64, LANES), bf16), vmem((2, HEADS, 64, LANES), bf16),
            vmem((2, HEADS, 64, LANES), bf16), vmem((2, HEADS, 64, LANES), bf16),
            vmem((HEADS, 64, LANES), bf16), vmem((HEADS, 64, LANES), bf16),
            dma((5,)), dma((2,)), dma((2,)),
            dma((1,)), dma((1,)), dma((1,)), dma((1,)), dma((1,)), dma((1,)), dma((1,)),
            dma((1,)), dma((2,)),
            dma((groups,)), dma((groups,)), dma((groups,)), dma((groups,)), dma((groups,)),
            dma((spans,)), dma((spans,)), dma((groups,)), dma((groups,)), dma((groups,)),
        ],
        compiler_params=pltpu.CompilerParams(
            collective_id=0, has_side_effects=True, vmem_limit_bytes=61 * 2**20
        ),
    )(
        queries.reshape(flat), keys.reshape(flat), values.reshape(flat),
        cotangent.reshape(flat), upstream.reshape(flat), block_mask.reshape(2, 9),
    )
    out = pl.pallas_call(
        store_kernel,
        out_shape=[jax.ShapeDtypeStruct(flat, bf16)] * 3,
        in_specs=[pl.BlockSpec(memory_space=pltpu.VMEM)] * 3,
        out_specs=[pl.BlockSpec(memory_space=pltpu.HBM)] * 3,
        scratch_shapes=[dma((3,))],
        compiler_params=pltpu.CompilerParams(vmem_limit_bytes=4 * 2**20),
    )(*out)
    return tuple(x.reshape(shape) for x in out)


def solution(mesh):
    return jax.shard_map(
        relay_body,
        mesh=mesh,
        in_specs=(
            P("section", None, "ha", "wa", None),
            P("section", None, "ha", "wa", None),
            P("section", None, "ha", "wa", None),
            P("section", None, "ha", "wa", None),
            P("section", None, "ha", "wa", None),
            P("section", "ha", "wa", None),
        ),
        out_specs=(
            P("section", None, "ha", "wa", None),
            P("section", None, "ha", "wa", None),
            P("section", None, "ha", "wa", None),
        ),
        check_vma=False,
    )
```

```python
import functools

import jax
import jax.numpy as jnp
from jax import lax
from jax.experimental import pallas as pl
from jax.experimental.pallas import tpu as pltpu
from jax.sharding import PartitionSpec as P

HEADS = 12
HEAD_DIM = 128
TILE = 8


NEG = -1e30
LANES = 128
GROUP = 2
SPAN = 4
LEAD = 4 // GROUP
FIRST = (0, 1)
SECOND = (6, 2, 7)
STEPS = (
    (0, 0, 8, 3), (0, 1, 9, 4), (0, 2, 10, 5), (1, 0, 11, -1), (0, 3, 12, -1), (1, 1, -1, -1),
    (0, 4, 13, -1), (1, 2, -1, -1), (0, 5, 14, -1), (1, 3, 15, -1), (1, 4, 16, -1), (1, 5, 17, -1),
)
MESH_ID = pl.DeviceIdType.MESH


def relay_kernel(
    sections, rows_n, cols_n,
    q_hbm, k_hbm, v_hbm, c_hbm, u_hbm, mask_hbm,
    oq_ref, ok_ref, ov_ref,
    q_ref, k_ref, v_ref, c_ref, mask_ref, handed,
    qb, gb, kb, vb, k_send, v_send, bias_send, bias, bias_tiles,
    weights, grads, tops, xs1, xr1,
    dq_own, dq_send, dq_recv, dk_own, dv_own, dk_send, dv_send, dk_recv, dv_recv, via_v, via_dv,
    load_sem, sec_sem, bias_sem, send_q, send_g, send_dq, send_k, send_v, send_dk, send_dv,
    send_x1, send_via, recv_q, recv_dq, recv_k, recv_dk,
    recv_x1, recv_via_v, recv_via_dv,
):
    f32, bf16 = jnp.float32, jnp.bfloat16
    sec = lax.axis_index("section")
    row = lax.axis_index("ha")
    col = lax.axis_index("wa")
    groups = HEADS // GROUP
    spans = HEADS // SPAN
    per_span = SPAN // GROUP
    inv_root = HEAD_DIM ** (-0.5)
    scale = inv_root * 1.4426950408889634
    has_up, has_down = row > 0, row < rows_n - 1
    has_up2, has_down2 = row > 1, row < rows_n - 2
    has_left, has_right = col > 0, col < cols_n - 1
    detour = cols_n == 4

    loads = [
        pltpu.make_async_copy(src, dst, load_sem.at[n])
        for n, (src, dst) in enumerate(
            ((q_hbm, q_ref), (k_hbm, k_ref), (v_hbm, v_ref), (mask_hbm, mask_ref), (c_hbm, c_ref))
        )
    ]
    for load in loads:
        load.start()

    barrier = pltpu.get_barrier_semaphore()
    greeted = [
        (has_up, {"ha": row - 1}),
        (has_down, {"ha": row + 1}),
        (has_up2, {"ha": row - 2}),
        (has_down2, {"ha": row + 2}),
        (has_left, {"wa": col - 1}),
        (has_right, {"wa": col + 1}),
        (sec > 0, {"section": sec - 1}),
        (sec < sections - 1, {"section": sec + 1}),
    ]
    if detour:
        greeted.append((col >= 0, {"wa": lax.rem(col + 2, 4)}))
    expected = jnp.int32(0)
    for cond, dev in greeted:
        @pl.when(cond)
        def _(dev=dev):
            pl.semaphore_signal(barrier, inc=1, device_id=dev, device_id_type=MESH_ID)

        expected = expected + cond.astype(jnp.int32)

    def remote(src, dst, send, recv, dev):
        return pltpu.make_async_remote_copy(
            src_ref=src, dst_ref=dst, send_sem=send, recv_sem=recv,
            device_id=dev, device_id_type=MESH_ID,
        )

    vertical = ((has_up, has_down, {"ha": row - 1}), (has_down, has_up, {"ha": row + 1}))
    sideways = ((has_left, has_right, {"wa": col - 1}), (has_right, has_left, {"wa": col + 1}))

    def slot_rows(d):
        return pl.ds(256 - 256 * d, 128)

    def halo_rows(side):
        return pl.ds(192 - 64 * side, 64)

    sec_copy = remote(u_hbm, handed, sec_sem.at[0], sec_sem.at[1], {"section": sec - 1})

    def bias_copy(d):
        return remote(
            bias_send.at[2 * d], bias.at[2 - 2 * d], bias_sem.at[0], bias_sem.at[1],
            vertical[d][2],
        )

    def rows_copy(buf, send, recv, d, heads, g):
        return remote(
            buf.at[heads, pl.ds(128, 128)], buf.at[heads, slot_rows(d)],
            send.at[0], recv.at[g], vertical[d][2],
        )

    def q_copy(d, g):
        return rows_copy(qb, send_q, recv_q, d, pl.ds(g * GROUP, GROUP), g)

    def g_copy(d, g):
        return rows_copy(gb, send_g, recv_q, d, pl.ds(g * GROUP, GROUP), g)

    def dq_copy(d, g):
        heads = pl.ds(g * GROUP, GROUP)
        return remote(
            dq_send.at[d, heads], dq_recv.at[1 - d, heads],
            send_dq.at[0], recv_dq.at[g], vertical[d][2],
        )

    def k_copy(side, heads, s):
        return remote(
            k_send.at[side, heads], kb.at[heads, halo_rows(side)],
            send_k.at[0], recv_k.at[s], sideways[side][2],
        )

    def v_copy(side, heads, s):
        return remote(
            v_send.at[side, heads], vb.at[heads, halo_rows(side)],
            send_v.at[0], recv_k.at[s], sideways[side][2],
        )

    def dk_copy(side, heads, s):
        return remote(
            dk_send.at[side, heads], dk_recv.at[1 - side, heads],
            send_dk.at[0], recv_dk.at[s], sideways[side][2],
        )

    def dv_copy(side, heads, s):
        return remote(
            dv_send.at[side, heads], dv_recv.at[1 - side, heads],
            send_dv.at[0], recv_dk.at[s], sideways[side][2],
        )

    def via_source(side):
        return col == (2, 1)[side]

    def via_holder(side):
        return col == (0, 3)[side]

    def via_v_in(side, heads, s):
        return remote(
            v_send.at[side, heads], via_v.at[heads], send_v.at[0], recv_via_v.at[s],
            {"wa": jnp.int32((0, 3)[side])},
        )

    def via_v_out(side, heads, s):
        return remote(
            via_v.at[heads], vb.at[heads, halo_rows(side)], send_via.at[0], recv_k.at[s],
            {"wa": jnp.int32((1, 2)[side])},
        )

    def via_dv_in(side, heads, g):
        return remote(
            dv_send.at[side, heads], via_dv.at[heads], send_dv.at[0], recv_via_dv.at[g],
            {"wa": jnp.int32((0, 3)[side])},
        )

    def via_dv_out(side, heads, s):
        return remote(
            via_dv.at[heads], dv_recv.at[1 - side, heads], send_via.at[1],
            recv_dk.at[s], {"wa": jnp.int32((1, 2)[side])},
        )

    stat_moves = (
        (has_up, has_down, {"ha": row - 1}, pl.ds(0, 2), pl.ds(2, 2)),
        (has_down, has_up, {"ha": row + 1}, pl.ds(1, 2), pl.ds(0, 2)),
        (has_up2, has_down2, {"ha": row - 2}, pl.ds(0, 1), pl.ds(5, 1)),
        (has_down2, has_up2, {"ha": row + 2}, pl.ds(2, 1), pl.ds(4, 1)),
    )

    def stat_copy(xs, xr, send, recv, m, g):
        _, _, dev, mine, theirs = stat_moves[m]
        return remote(xs.at[g, mine], xr.at[g, theirs], send.at[0], recv.at[g], dev)

    def stat_start(xs, xr, send, recv, g):
        for m in range(4):
            @pl.when(stat_moves[m][0])
            def _(m=m):
                stat_copy(xs, xr, send, recv, m, g).start()

    def stat_tiles(at):
        return 2 * ((at > 0) + (at < rows_n - 1)) + (at > 1) + (at < rows_n - 2)

    tiles_here = sum(
        n * cond.astype(jnp.int32)
        for n, cond in ((2, has_up), (2, has_down), (1, has_up2), (1, has_down2))
    )

    def stat_wait(xr, sem, g):
        for tiles in sorted({stat_tiles(at) for at in range(rows_n)} - {0}):
            @pl.when(tiles_here == tiles)
            def _(tiles=tiles):
                ref = xr.at[g, pl.ds(0, tiles)]
                pltpu.make_async_copy(ref, ref, sem).wait()

    def wait_pair(first, second, ref_both, ref_one, sem):
        @pl.when(first & second)
        def _():
            pltpu.make_async_copy(ref_both, ref_both, sem).wait()

        @pl.when(first ^ second)
        def _():
            pltpu.make_async_copy(ref_one, ref_one, sem).wait()

    def wait_rows(buf, sem, heads):
        wait_pair(
            has_up, has_down, buf.at[heads, pl.ds(0, 256)], buf.at[heads, pl.ds(0, 128)], sem
        )

    def wait_halos(buf, sem, heads):
        wait_pair(
            has_left, has_right, buf.at[heads, pl.ds(128, 128)], buf.at[heads, pl.ds(128, 64)], sem
        )

    def wait_two(buf, sem, heads, first, second):
        wait_pair(first, second, buf.at[:, heads], buf.at[0, heads], sem)

    def issue(chunk):
        kind, g = lax.div(chunk, groups), lax.rem(chunk, groups)
        for d in range(2):
            for n, copy in enumerate((q_copy, g_copy, dq_copy)):
                @pl.when(vertical[d][0] & (chunk >= 0) & (kind == n))
                def _(d=d, copy=copy):
                    copy(d, g).start()

    def head_cols(head):
        return pl.ds(pl.multiple_of(head * LANES, LANES), LANES)

    def split(block):
        tiles = block.astype(f32).reshape(8, 2, 8, LANES)
        return [tiles[:, t].reshape(64, LANES).astype(bf16) for t in range(2)]

    def spread(ref, buf, send):
        @pl.loop(0, HEADS)
        def _(h):
            block = ref[:, head_cols(h)]
            buf[h, pl.ds(0, 128)] = block
            for side, part in enumerate(split(block)):
                send[side, h] = part

    loads[0].wait()

    @pl.loop(0, HEADS)
    def _(h):
        qb[h, pl.ds(128, 128)] = q_ref[:, head_cols(h)]

    pl.semaphore_wait(barrier, expected)

    issue(jnp.int32(FIRST[0]))
    @pl.when(sec > 0)
    def _():
        sec_copy.start()

    for chunk in FIRST[1:]:
        issue(jnp.int32(chunk))

    def start_k(g):
        for side in range(2):
            @pl.when(sideways[side][0])
            def _(side=side):
                k_copy(side, pl.ds(g * GROUP, GROUP), g).start()

    def start_v(g):
        heads = pl.ds(g * GROUP, GROUP)
        for side in range(2):
            if detour:
                @pl.when(via_source(side))
                def _(side=side):
                    via_v_in(side, heads, g).start()

            @pl.when(sideways[side][0] & ~via_source(side) if detour else sideways[side][0])
            def _(side=side):
                v_copy(side, heads, g).start()

    def start_kv(g):
        start_k(g)
        start_v(g)

    def forward_v(g):
        for side in range(2):
            @pl.when(via_holder(side))
            def _(side=side):
                heads = pl.ds(g * GROUP, GROUP)
                via_v_in(side, heads, g).wait_recv()
                via_v_out(side, heads, g).start()

    def forward_dv(g):
        for side in range(2):
            @pl.when(via_holder(side))
            def _(side=side):
                heads = pl.ds(g * GROUP, GROUP)
                via_dv_in(side, heads, g).wait_recv()
                via_dv_out(side, heads, lax.div(g, per_span)).start()

    loads[1].wait()
    spread(k_ref, kb, k_send)
    for g in range(LEAD):
        start_k(g)

    loads[3].wait()
    lane = lax.broadcasted_iota(jnp.int32, (1, LANES), 1)
    first_tile = lax.rem(lane // TILE, 2) == 0
    dead = jnp.int32(0)
    left = jnp.where(has_left, 1, 0)
    right = jnp.where(has_right, 1, 0)
    for i in range(3):
        entry = [[mask_ref[t, 3 * i + j] for j in range(3)] for t in range(2)]
        for n, (first, second) in enumerate((
            (entry[0][1], entry[1][0]),
            (entry[0][2], entry[1][1]),
            (entry[0][0] * left, dead),
            (dead, entry[1][2] * right),
        )):
            seen = jnp.where(first_tile, first, second)
            bias_send[i, pl.ds(n, 1)] = jnp.where(seen > 0, 0.0, NEG).astype(f32)
    bias[1] = bias_send[1]

    for d in range(2):
        @pl.when(vertical[d][0])
        def _(d=d):
            bias_copy(d).start()

    loads[2].wait()
    spread(v_ref, vb, v_send)
    for g in range(LEAD):
        start_v(g)

    for cond, at in ((row == 0, 0), (row == rows_n - 1, 256)):
        @pl.when(cond)
        def _(at=at):
            bias[2 * at // 256] = jnp.zeros((4, LANES), f32)

            @pl.loop(0, HEADS)
            def _(h):
                qb[h, pl.ds(at, 128)] = jnp.zeros((128, LANES), bf16)
                gb[h, pl.ds(at, 128)] = jnp.zeros((128, LANES), bf16)
                dq_recv[at // 256, h] = jnp.zeros((128, LANES), bf16)

    for cond, side in ((col == 0, 0), (col == cols_n - 1, 1)):
        @pl.when(cond)
        def _(side=side):
            @pl.loop(0, HEADS)
            def _(h):
                kb[h, pl.ds(128 + 64 * side, 64)] = jnp.zeros((64, LANES), bf16)
                vb[h, pl.ds(128 + 64 * side, 64)] = jnp.zeros((64, LANES), bf16)
                dk_recv[side, h] = jnp.zeros((64, LANES), bf16)
                dv_recv[side, h] = jnp.zeros((64, LANES), bf16)

    stat_row = lax.broadcasted_iota(jnp.int32, (2 * GROUP, LANES), 0)
    no_stat = jnp.where(stat_row < GROUP, NEG, 0.0).astype(f32)
    for cond, pieces in (
        (row == 0, (0, 1)), (row < 2, (4,)),
        (row == rows_n - 1, (2, 3)), (row > rows_n - 3, (5,)),
    ):
        @pl.when(cond)
        def _(pieces=pieces):
            for g in range(groups):
                for piece in pieces:
                    xr1[g, piece] = no_stat

    @pl.when(sec == sections - 1)
    def _():
        handed[...] = jnp.zeros_like(handed)

    @pl.when(sec < sections - 1)
    def _():
        sec_copy.wait_recv()

    loads[4].wait()

    @pl.loop(0, HEADS)
    def _(h):
        at = head_cols(h)
        gb[h, pl.ds(128, 128)] = (c_ref[:, at].astype(f32) + handed[:, at].astype(f32)).astype(bf16)

    for chunk in SECOND:
        issue(jnp.int32(chunk))

    for g in range(LEAD):
        if detour:
            forward_v(g)
        start_kv(g + LEAD)

    wait_pair(has_up, has_down, bias.at[pl.ds(0, 2)], bias.at[0], bias_sem.at[1])
    for n in range(3):
        for k in range(4):
            bias_tiles[n, k] = jnp.broadcast_to(bias[n, pl.ds(k, 1)], (8, LANES))

    nt = (((1,), (1,)), ((), ()))
    nn = (((1,), (0,)), ((), ()))
    tn = (((0,), (0,)), ((), ()))

    def dot(a, b, dims):
        return lax.dot_general(a, b, dims, preferred_element_type=f32)

    slots = [slice(n * 128, n * 128 + 128) for n in range(3)]

    def exponents(g, first, second):
        heads = pl.ds(g * GROUP, GROUP)
        wait_rows(qb, recv_q.at[g], pl.ds(0, 2 * GROUP))
        wait_halos(kb, recv_k.at[g], pl.ds(0, 2 * GROUP))
        for i in range(GROUP):
            h = g * GROUP + i
            part = dot(kb[h], qb[h], nt)
            grad_part = dot(vb[h], gb[h], nt)
            for n, at in enumerate(slots):
                rows = part[:, at] * scale
                scores = jnp.concatenate(
                    [
                        (rows[:128].reshape(8, 2, 8, LANES) + bias_tiles[n, 0:2][None]).reshape(128, LANES),
                        (rows[128:192].reshape(8, 8, LANES) + bias_tiles[n, 2][None]).reshape(64, LANES),
                        (rows[192:].reshape(8, 8, LANES) + bias_tiles[n, 3][None]).reshape(64, LANES),
                    ],
                    axis=0,
                )
                top = jnp.max(scores, axis=0, keepdims=True)
                exps = jnp.exp2(scores - top)
                weights[h, :, at] = exps
                grads[h, :, at] = grad_part[:, at]
                total = jnp.sum(exps, axis=0, keepdims=True)
                delta = jnp.sum(exps * grad_part[:, at], axis=0, keepdims=True)
                tops[g, n, pl.ds(i, 1)] = top
                xs1[g, n, pl.ds(i, 1)] = top + jnp.log(total) * 1.4426950408889634
                xs1[g, n, pl.ds(GROUP + i, 1)] = delta / total

        stat_start(xs1, xr1, send_x1, recv_x1, g)
        issue(first)
        issue(second)

        @pl.when(g + LEAD < groups)
        def _():
            if detour:
                forward_v(g + LEAD)

            @pl.when(g + 2 * LEAD < groups)
            def _():
                start_kv(g + 2 * LEAD)

    others = ((0, 4), (1, 2), (3, 5))

    def gradients(g, first, second):
        stat_wait(xr1, recv_x1.at[g], g)
        factors, deltas = [], []
        for n in range(3):
            stats = [xs1[g, n], xr1[g, others[n][0]], xr1[g, others[n][1]]]
            top = jnp.maximum(
                jnp.maximum(stats[0][:GROUP], stats[1][:GROUP]), stats[2][:GROUP]
            )
            shares = [jnp.exp2(stat[:GROUP] - top) for stat in stats]
            inverse = 1.0 / (shares[0] + shares[1] + shares[2])
            delta = sum(share * stat[GROUP:] for share, stat in zip(shares, stats))
            factors.append(jnp.exp2(tops[g, n, pl.ds(0, GROUP)] - top) * inverse)
            deltas.append(delta * inverse)
        pairs = []
        for i in range(GROUP):
            h = g * GROUP + i
            lows, scores = [], []
            for n, at in enumerate(slots):
                probs = weights[h, :, at] * factors[n][i:i + 1]
                lows.append(probs.astype(bf16))
                scores.append((probs * (grads[h, :, at] - deltas[n][i:i + 1]) * inv_root).astype(bf16))
            low = jnp.concatenate(lows, axis=1)
            score = jnp.concatenate(scores, axis=1)
            pairs.append((h, low, score))
            grad_query = dot(score, kb[h], tn)
            dq_send[0, h] = grad_query[:128].astype(bf16)
            dq_own[h] = grad_query[128:256]
            dq_send[1, h] = grad_query[256:].astype(bf16)

        issue(first)
        issue(second)
        for h, low, score in pairs:
            grad_value = dot(low, gb[h], nn)
            dv_own[h] = grad_value[:128]
            dv_send[0, h] = grad_value[128:192].astype(bf16)
            dv_send[1, h] = grad_value[192:].astype(bf16)
            grad_key = dot(score, qb[h], nn)
            dk_own[h] = grad_key[:128]
            dk_send[0, h] = grad_key[128:192].astype(bf16)
            dk_send[1, h] = grad_key[192:].astype(bf16)

        heads = pl.ds(g * GROUP, GROUP)
        s = lax.div(g, per_span)
        for side in range(2):
            around = via_source(side) & (g < groups - 1) if detour else None
            if detour:
                @pl.when(around)
                def _(side=side):
                    via_dv_in(side, heads, g).start()

            @pl.when(sideways[side][0] & ~around if detour else sideways[side][0])
            def _(side=side):
                dv_copy(side, heads, s).start()

            @pl.when(sideways[side][0])
            def _(side=side):
                dk_copy(side, heads, s).start()

        if detour:
            @pl.when(g > 0)
            def _():
                forward_dv(g - 1)

    @pl.loop(0, len(STEPS))
    def _(t):
        stage, g, first, second = (
            sum((t == n).astype(jnp.int32) * step[at] for n, step in enumerate(STEPS))
            for at in range(4)
        )
        for n, run in enumerate((exponents, gradients)):
            @pl.when(stage == n)
            def _(run=run):
                run(g, first, second)

    def fold(own, recv, h):
        blocks = own[h].reshape(8, 2, 8, LANES)
        sides = [recv[side, h].astype(f32).reshape(8, 1, 8, LANES) for side in range(2)]
        return (blocks + jnp.concatenate(sides, axis=1)).reshape(128, LANES).astype(bf16)

    def finish_keys(s):
        wait_two(dk_recv, recv_dk.at[s], pl.ds(0, 2 * SPAN), has_left, has_right)
        for i in range(SPAN):
            h = s * SPAN + i
            ov_ref[:, head_cols(h)] = fold(dv_own, dv_recv, h)
            ok_ref[:, head_cols(h)] = fold(dk_own, dk_recv, h)

    def finish_queries(g):
        heads = pl.ds(g * GROUP, GROUP)
        wait_two(dq_recv, recv_dq.at[g], heads, has_up, has_down)
        for i in range(GROUP):
            h = g * GROUP + i
            oq_ref[:, head_cols(h)] = (
                dq_own[h] + dq_recv[0, h].astype(f32) + dq_recv[1, h].astype(f32)
            ).astype(bf16)

    @pl.loop(0, spans - 1)
    def _(s):
        finish_keys(s)

    @pl.loop(0, groups - 1)
    def _(g):
        finish_queries(g)

    finish_keys(spans - 1)
    finish_queries(groups - 1)

    @pl.when(sec > 0)
    def _():
        sec_copy.wait_send()

    every = pl.ds(0, HEADS)
    wait_pair(has_up, has_down, bias.at[pl.ds(0, 2)], bias.at[0], bias_sem.at[0])
    wait_rows(qb, send_q.at[0], every)
    wait_rows(gb, send_g.at[0], every)
    wait_two(dq_send, send_dq.at[0], every, has_up, has_down)
    stat_wait(xr1, send_x1.at[0], pl.ds(0, groups))
    for buf, sem in ((k_send, send_k), (v_send, send_v), (dk_send, send_dk), (dv_send, send_dv)):
        wait_two(buf, sem.at[0], every, has_left, has_right)
    if detour:
        for side in range(2):
            @pl.when(via_holder(side))
            def _(side=side):
                via_v_out(side, every, 0).wait_send()
                via_dv_out(side, pl.ds(0, HEADS - GROUP), 0).wait_send()


def store_kernel(aq, ak, av, oq, ok, ov, sems):
    stores = [
        pltpu.make_async_copy(src, dst, sems.at[n])
        for n, (src, dst) in enumerate(((aq, oq), (ak, ok), (av, ov)))
    ]
    for store in stores:
        store.start()
    for store in stores:
        store.wait()


def relay_body(queries, keys, values, cotangent, upstream, block_mask):
    sections, rows_n, cols_n = (lax.axis_size(a) for a in ("section", "ha", "wa"))
    shape = queries.shape
    tokens = shape[1] * shape[2] * shape[3]
    flat = (tokens, shape[4])
    groups, spans = HEADS // GROUP, HEADS // SPAN
    bf16, f32 = jnp.bfloat16, jnp.float32
    dma = pltpu.SemaphoreType.DMA
    vmem = pltpu.VMEM
    out = pl.pallas_call(
        functools.partial(relay_kernel, sections, rows_n, cols_n),
        out_shape=[vmem(flat, bf16)] * 3,
        in_specs=[pl.BlockSpec(memory_space=pltpu.HBM)] * 6,
        out_specs=[pl.BlockSpec(memory_space=pltpu.VMEM)] * 3,
        scratch_shapes=[
            vmem(flat, bf16), vmem(flat, bf16), vmem(flat, bf16), vmem(flat, bf16),
            pltpu.SMEM((2, 9), jnp.int32),
            vmem(flat, bf16),
            vmem((HEADS, 384, LANES), bf16), vmem((HEADS, 384, LANES), bf16),
            vmem((HEADS, 256, LANES), bf16), vmem((HEADS, 256, LANES), bf16),
            vmem((2, HEADS, 64, LANES), bf16), vmem((2, HEADS, 64, LANES), bf16),
            vmem((3, 4, LANES), f32), vmem((3, 4, LANES), f32), vmem((3, 4, 8, LANES), f32),
            vmem((HEADS, 256, 384), f32), vmem((HEADS, 256, 384), f32),
            vmem((groups, 3, 8, LANES), f32),
            vmem((groups, 3, 2 * GROUP, LANES), f32), vmem((groups, 6, 2 * GROUP, LANES), f32),
            vmem((HEADS, 128, LANES), f32),
            vmem((2, HEADS, 128, LANES), bf16), vmem((2, HEADS, 128, LANES), bf16),
            vmem((HEADS, 128, LANES), f32), vmem((HEADS, 128, LANES), f32),
            vmem((2, HEADS, 64, LANES), bf16), vmem((2, HEADS, 64, LANES), bf16),
            vmem((2, HEADS, 64, LANES), bf16), vmem((2, HEADS, 64, LANES), bf16),
            vmem((HEADS, 64, LANES), bf16), vmem((HEADS, 64, LANES), bf16),
            dma((5,)), dma((2,)), dma((2,)),
            dma((1,)), dma((1,)), dma((1,)), dma((1,)), dma((1,)), dma((1,)), dma((1,)),
            dma((1,)), dma((2,)),
            dma((groups,)), dma((groups,)), dma((groups,)), dma((spans,)),
            dma((groups,)), dma((groups,)), dma((groups,)),
        ],
        compiler_params=pltpu.CompilerParams(
            collective_id=0, has_side_effects=True, vmem_limit_bytes=61 * 2**20
        ),
    )(
        queries.reshape(flat), keys.reshape(flat), values.reshape(flat),
        cotangent.reshape(flat), upstream.reshape(flat), block_mask.reshape(2, 9),
    )
    out = pl.pallas_call(
        store_kernel,
        out_shape=[jax.ShapeDtypeStruct(flat, bf16)] * 3,
        in_specs=[pl.BlockSpec(memory_space=pltpu.VMEM)] * 3,
        out_specs=[pl.BlockSpec(memory_space=pltpu.HBM)] * 3,
        scratch_shapes=[dma((3,))],
        compiler_params=pltpu.CompilerParams(vmem_limit_bytes=4 * 2**20),
    )(*out)
    return tuple(x.reshape(shape) for x in out)


def solution(mesh):
    return jax.shard_map(
        relay_body,
        mesh=mesh,
        in_specs=(
            P("section", None, "ha", "wa", None),
            P("section", None, "ha", "wa", None),
            P("section", None, "ha", "wa", None),
            P("section", None, "ha", "wa", None),
            P("section", None, "ha", "wa", None),
            P("section", "ha", "wa", None),
        ),
        out_specs=(
            P("section", None, "ha", "wa", None),
            P("section", None, "ha", "wa", None),
            P("section", None, "ha", "wa", None),
        ),
        check_vma=False,
    )
```

```python
import functools

import jax
import jax.numpy as jnp
from jax import lax
from jax.experimental import pallas as pl
from jax.experimental.pallas import tpu as pltpu
from jax.sharding import PartitionSpec as P

HEADS = 12
HEAD_DIM = 128
TILE = 8


NEG = -1e30
LANES = 128
GROUP = 2
LEAD = 2
FIRST = (0, 1)
SECOND = (6, 2, 7, 8)
STEPS = (
    (0, 0, 3, 9), (0, 1, 10, -1), (0, 2, 4, 5), (1, 0, 11, -1), (0, 3, -1, -1), (1, 1, 12, -1),
    (0, 4, -1, -1), (1, 2, 13, -1), (0, 5, 14, -1), (1, 3, 15, -1), (1, 4, 16, -1), (1, 5, 17, -1),
)
VIA_KV = (1, 3, 5)
VIA_GRAD = (0, 2, 4)
MESH_ID = pl.DeviceIdType.MESH


def relay_kernel(
    sections, rows_n, cols_n,
    q_hbm, k_hbm, v_hbm, c_hbm, u_hbm, mask_hbm,
    oq_ref, ok_ref, ov_ref,
    q_ref, k_ref, v_ref, c_ref, mask_ref, handed,
    qb, gb, kv, kv_send, bias_send, bias, bias_tiles,
    weights, grads, tops, xs1, xr1,
    dq_own, dq_send, dq_recv, dk_own, dv_own, dkv_send, dkv_recv, via_kv, via_dkv,
    load_sem, sec_sem, bias_sem, send_q, send_g, send_dq, send_kv, send_dkv, send_x1, send_via,
    recv_q, recv_dq, recv_kv, recv_dkv, recv_x1, recv_via,
):
    f32, bf16 = jnp.float32, jnp.bfloat16
    sec = lax.axis_index("section")
    row = lax.axis_index("ha")
    col = lax.axis_index("wa")
    groups = HEADS // GROUP
    inv_root = HEAD_DIM ** (-0.5)
    scale = inv_root * 1.4426950408889634
    has_up, has_down = row > 0, row < rows_n - 1
    has_up2, has_down2 = row > 1, row < rows_n - 2
    has_left, has_right = col > 0, col < cols_n - 1
    detour = cols_n == 4

    ahead, rest = pl.ds(0, GROUP * LANES), pl.ds(GROUP * LANES, (HEADS - GROUP) * LANES)
    loads = [
        pltpu.make_async_copy(src, dst, load_sem.at[n])
        for n, (src, dst) in enumerate(
            (
                (q_hbm.at[:, ahead], q_ref.at[:, ahead]), (k_hbm, k_ref), (v_hbm, v_ref),
                (mask_hbm, mask_ref), (c_hbm, c_ref), (q_hbm.at[:, rest], q_ref.at[:, rest]),
            )
        )
    ]
    for n in (0, 5, 1, 2, 3, 4):
        loads[n].start()

    barrier = pltpu.get_barrier_semaphore()
    greeted = [
        (has_up, {"ha": row - 1}),
        (has_down, {"ha": row + 1}),
        (has_up2, {"ha": row - 2}),
        (has_down2, {"ha": row + 2}),
        (has_left, {"wa": col - 1}),
        (has_right, {"wa": col + 1}),
        (sec > 0, {"section": sec - 1}),
        (sec < sections - 1, {"section": sec + 1}),
    ]
    if detour:
        greeted.append((col >= 0, {"wa": lax.rem(col + 2, 4)}))
    expected = jnp.int32(0)
    for cond, dev in greeted:
        @pl.when(cond)
        def _(dev=dev):
            pl.semaphore_signal(barrier, inc=1, device_id=dev, device_id_type=MESH_ID)

        expected = expected + cond.astype(jnp.int32)

    def remote(src, dst, send, recv, dev):
        return pltpu.make_async_remote_copy(
            src_ref=src, dst_ref=dst, send_sem=send, recv_sem=recv,
            device_id=dev, device_id_type=MESH_ID,
        )

    vertical = ((has_up, has_down, {"ha": row - 1}), (has_down, has_up, {"ha": row + 1}))
    sideways = ((has_left, has_right, {"wa": col - 1}), (has_right, has_left, {"wa": col + 1}))

    def slot_rows(d):
        return pl.ds(256 - 256 * d, 128)

    def halo_rows(side):
        return pl.ds(192 - 64 * side, 64)

    sec_copy = remote(u_hbm, handed, sec_sem.at[0], sec_sem.at[1], {"section": sec - 1})

    def bias_copy(d):
        return remote(
            bias_send.at[2 * d], bias.at[2 - 2 * d], bias_sem.at[0], bias_sem.at[1],
            vertical[d][2],
        )

    def rows_copy(buf, send, recv, d, heads, g):
        return remote(
            buf.at[heads, pl.ds(128, 128)], buf.at[heads, slot_rows(d)],
            send.at[0], recv.at[g], vertical[d][2],
        )

    def q_copy(d, g):
        return rows_copy(qb, send_q, recv_q, d, pl.ds(g * GROUP, GROUP), g)

    def g_copy(d, g):
        return rows_copy(gb, send_g, recv_q, d, pl.ds(g * GROUP, GROUP), g)

    def dq_copy(d, g):
        heads = pl.ds(g * GROUP, GROUP)
        return remote(
            dq_send.at[d, heads], dq_recv.at[1 - d, heads],
            send_dq.at[0], recv_dq.at[g], vertical[d][2],
        )

    def kv_copy(side, g):
        heads = pl.ds(g * GROUP, GROUP)
        return remote(
            kv_send.at[side, :, heads], kv.at[:, heads, halo_rows(side)],
            send_kv.at[0], recv_kv.at[g], sideways[side][2],
        )

    def grad_copy(side, g):
        heads = pl.ds(g * GROUP, GROUP)
        return remote(
            dkv_send.at[side, :, heads], dkv_recv.at[1 - side, :, heads],
            send_dkv.at[0], recv_dkv.at[g], sideways[side][2],
        )

    def via_source(side):
        return col == (2, 1)[side]

    def via_holder(side):
        return col == (0, 3)[side]

    def via_kv_in(side, g):
        heads = pl.ds(g * GROUP, GROUP)
        return remote(
            kv_send.at[side, :, heads], via_kv.at[:, heads], send_kv.at[0], recv_via.at[0, g],
            {"wa": jnp.int32((0, 3)[side])},
        )

    def via_kv_out(side, g):
        heads = pl.ds(g * GROUP, GROUP)
        return remote(
            via_kv.at[:, heads], kv.at[:, heads, halo_rows(side)], send_via.at[0], recv_kv.at[g],
            {"wa": jnp.int32((1, 2)[side])},
        )

    def via_grad_in(side, g):
        heads = pl.ds(g * GROUP, GROUP)
        return remote(
            dkv_send.at[side, :, heads], via_dkv.at[:, heads], send_dkv.at[0], recv_via.at[1, g],
            {"wa": jnp.int32((0, 3)[side])},
        )

    def via_grad_out(side, g):
        heads = pl.ds(g * GROUP, GROUP)
        return remote(
            via_dkv.at[:, heads], dkv_recv.at[1 - side, :, heads], send_via.at[1], recv_dkv.at[g],
            {"wa": jnp.int32((1, 2)[side])},
        )

    def is_in(g, names):
        return sum((g == n).astype(jnp.int32) for n in names) > 0

    def start_side(names, copy, inward, g):
        g = jnp.int32(g)
        for side in range(2):
            if detour:
                around = via_source(side) & is_in(g, names)

                @pl.when(around)
                def _(side=side):
                    inward(side, g).start()

                @pl.when(sideways[side][0] & ~around)
                def _(side=side):
                    copy(side, g).start()
            else:
                @pl.when(sideways[side][0])
                def _(side=side):
                    copy(side, g).start()

    def forward(names, inward, outward, g):
        g = jnp.int32(g)
        if detour:
            for side in range(2):
                @pl.when(via_holder(side) & is_in(g, names))
                def _(side=side):
                    inward(side, g).wait_recv()
                    outward(side, g).start()

    def start_kv(g):
        start_side(VIA_KV, kv_copy, via_kv_in, g)

    def start_grad(g):
        start_side(VIA_GRAD, grad_copy, via_grad_in, g)

    def forward_kv(g):
        forward(VIA_KV, via_kv_in, via_kv_out, g)

    def forward_grad(g):
        forward(VIA_GRAD, via_grad_in, via_grad_out, g)

    stat_moves = (
        (has_up, has_down, {"ha": row - 1}, pl.ds(0, 2), pl.ds(2, 2)),
        (has_down, has_up, {"ha": row + 1}, pl.ds(1, 2), pl.ds(0, 2)),
        (has_up2, has_down2, {"ha": row - 2}, pl.ds(0, 1), pl.ds(5, 1)),
        (has_down2, has_up2, {"ha": row + 2}, pl.ds(2, 1), pl.ds(4, 1)),
    )

    def stat_copy(xs, xr, send, recv, m, g):
        _, _, dev, mine, theirs = stat_moves[m]
        return remote(xs.at[g, mine], xr.at[g, theirs], send.at[0], recv.at[g], dev)

    def stat_start(xs, xr, send, recv, g):
        for m in range(4):
            @pl.when(stat_moves[m][0])
            def _(m=m):
                stat_copy(xs, xr, send, recv, m, g).start()

    def stat_tiles(at):
        return 2 * ((at > 0) + (at < rows_n - 1)) + (at > 1) + (at < rows_n - 2)

    tiles_here = sum(
        n * cond.astype(jnp.int32)
        for n, cond in ((2, has_up), (2, has_down), (1, has_up2), (1, has_down2))
    )

    def stat_wait(xr, sem, g):
        for tiles in sorted({stat_tiles(at) for at in range(rows_n)} - {0}):
            @pl.when(tiles_here == tiles)
            def _(tiles=tiles):
                ref = xr.at[g, pl.ds(0, tiles)]
                pltpu.make_async_copy(ref, ref, sem).wait()

    def wait_pair(first, second, ref_both, ref_one, sem):
        @pl.when(first & second)
        def _():
            pltpu.make_async_copy(ref_both, ref_both, sem).wait()

        @pl.when(first ^ second)
        def _():
            pltpu.make_async_copy(ref_one, ref_one, sem).wait()

    def wait_rows(buf, sem, heads):
        wait_pair(
            has_up, has_down, buf.at[heads, pl.ds(0, 256)], buf.at[heads, pl.ds(0, 128)], sem
        )

    def wait_halos(buf, sem, heads):
        wait_pair(has_left, has_right, buf.at[:, :, heads], buf.at[0, :, heads], sem)

    def wait_two(buf, sem, heads, first, second):
        wait_pair(first, second, buf.at[:, heads], buf.at[0, heads], sem)

    def issue(chunk):
        kind, g = lax.div(chunk, groups), lax.rem(chunk, groups)

        @pl.when(chunk >= 0)
        def _():
            for n, copy in enumerate((q_copy, g_copy, dq_copy)):
                @pl.when(kind == n)
                def _(copy=copy):
                    for d in range(2):
                        @pl.when(vertical[d][0])
                        def _(d=d):
                            copy(d, g).start()

    def head_cols(head):
        return pl.ds(pl.multiple_of(head * LANES, LANES), LANES)

    def split(block):
        tiles = block.astype(f32).reshape(8, 2, 8, LANES)
        return [tiles[:, t].reshape(64, LANES).astype(bf16) for t in range(2)]

    def spread(ref, n):
        @pl.loop(0, HEADS)
        def _(h):
            block = ref[:, head_cols(h)]
            kv[n, h, pl.ds(0, 128)] = block
            for side, part in enumerate(split(block)):
                kv_send[side, n, h] = part

    loads[0].wait()

    def place_q(h):
        qb[h, pl.ds(128, 128)] = q_ref[:, head_cols(h)]

    for h in range(GROUP):
        place_q(h)

    pl.semaphore_wait(barrier, expected)

    issue(jnp.int32(FIRST[0]))
    loads[5].wait()
    pl.loop(GROUP, HEADS)(place_q)

    @pl.when(sec > 0)
    def _():
        sec_copy.start()

    for chunk in FIRST[1:]:
        issue(jnp.int32(chunk))

    loads[1].wait()
    spread(k_ref, 0)
    loads[2].wait()
    spread(v_ref, 1)
    for g in range(LEAD):
        start_kv(g)


    loads[3].wait()
    lane = lax.broadcasted_iota(jnp.int32, (1, LANES), 1)
    first_tile = lax.rem(lane // TILE, 2) == 0
    dead = jnp.int32(0)
    left = jnp.where(has_left, 1, 0)
    right = jnp.where(has_right, 1, 0)
    for i in range(3):
        entry = [[mask_ref[t, 3 * i + j] for j in range(3)] for t in range(2)]
        for n, (first, second) in enumerate((
            (entry[0][1], entry[1][0]),
            (entry[0][2], entry[1][1]),
            (entry[0][0] * left, dead),
            (dead, entry[1][2] * right),
        )):
            seen = jnp.where(first_tile, first, second)
            bias_send[i, pl.ds(n, 1)] = jnp.where(seen > 0, 0.0, NEG).astype(f32)
    bias[1] = bias_send[1]

    for d in range(2):
        @pl.when(vertical[d][0])
        def _(d=d):
            bias_copy(d).start()


    for cond, at in ((row == 0, 0), (row == rows_n - 1, 256)):
        @pl.when(cond)
        def _(at=at):
            bias[2 * at // 256] = jnp.zeros((4, LANES), f32)

            @pl.loop(0, HEADS)
            def _(h):
                qb[h, pl.ds(at, 128)] = jnp.zeros((128, LANES), bf16)
                gb[h, pl.ds(at, 128)] = jnp.zeros((128, LANES), bf16)
                dq_recv[at // 256, h] = jnp.zeros((128, LANES), bf16)

    for cond, side in ((col == 0, 0), (col == cols_n - 1, 1)):
        @pl.when(cond)
        def _(side=side):
            @pl.loop(0, HEADS)
            def _(h):
                for n in range(2):
                    kv[n, h, pl.ds(128 + 64 * side, 64)] = jnp.zeros((64, LANES), bf16)
                    dkv_recv[side, n, h] = jnp.zeros((64, LANES), bf16)

    stat_row = lax.broadcasted_iota(jnp.int32, (2 * GROUP, LANES), 0)
    no_stat = jnp.where(stat_row < GROUP, NEG, 0.0).astype(f32)
    for cond, pieces in (
        (row == 0, (0, 1)), (row < 2, (4,)),
        (row == rows_n - 1, (2, 3)), (row > rows_n - 3, (5,)),
    ):
        @pl.when(cond)
        def _(pieces=pieces):
            for g in range(groups):
                for piece in pieces:
                    xr1[g, piece] = no_stat

    @pl.when(sec == sections - 1)
    def _():
        handed[...] = jnp.zeros_like(handed)

    @pl.when(sec < sections - 1)
    def _():
        sec_copy.wait_recv()

    loads[4].wait()

    @pl.loop(0, HEADS)
    def _(h):
        at = head_cols(h)
        gb[h, pl.ds(128, 128)] = (c_ref[:, at].astype(f32) + handed[:, at].astype(f32)).astype(bf16)

    for chunk in SECOND:
        issue(jnp.int32(chunk))

    for g in range(LEAD):
        forward_kv(g)
        start_kv(g + LEAD)

    wait_pair(has_up, has_down, bias.at[pl.ds(0, 2)], bias.at[0], bias_sem.at[1])
    for n in range(3):
        for k in range(4):
            bias_tiles[n, k] = jnp.broadcast_to(bias[n, pl.ds(k, 1)], (8, LANES))

    nt = (((1,), (1,)), ((), ()))
    nn = (((1,), (0,)), ((), ()))
    tn = (((0,), (0,)), ((), ()))

    def dot(a, b, dims):
        return lax.dot_general(a, b, dims, preferred_element_type=f32)

    slots = [slice(n * 128, n * 128 + 128) for n in range(3)]

    def exponents(g, first, second):
        heads = pl.ds(g * GROUP, GROUP)
        wait_rows(qb, recv_q.at[g], pl.ds(0, 2 * GROUP))
        wait_halos(kv_send, recv_kv.at[g], heads)
        for i in range(GROUP):
            h = g * GROUP + i
            part = dot(kv[0, h], qb[h], nt)
            grad_part = dot(kv[1, h], gb[h], nt)
            for n, at in enumerate(slots):
                rows = part[:, at] * scale
                scores = jnp.concatenate(
                    [
                        (rows[:128].reshape(8, 2, 8, LANES) + bias_tiles[n, 0:2][None]).reshape(128, LANES),
                        (rows[128:192].reshape(8, 8, LANES) + bias_tiles[n, 2][None]).reshape(64, LANES),
                        (rows[192:].reshape(8, 8, LANES) + bias_tiles[n, 3][None]).reshape(64, LANES),
                    ],
                    axis=0,
                )
                top = jnp.max(scores, axis=0, keepdims=True)
                exps = jnp.exp2(scores - top)
                weights[h, :, at] = exps
                grads[h, :, at] = grad_part[:, at]
                total = jnp.sum(exps, axis=0, keepdims=True)
                delta = jnp.sum(exps * grad_part[:, at], axis=0, keepdims=True)
                tops[g, n, pl.ds(i, 1)] = top
                xs1[g, n, pl.ds(i, 1)] = top + jnp.log(total) * 1.4426950408889634
                xs1[g, n, pl.ds(GROUP + i, 1)] = delta / total

        stat_start(xs1, xr1, send_x1, recv_x1, g)
        issue(first)
        issue(second)

        @pl.when(g + LEAD < groups)
        def _():
            forward_kv(g + LEAD)

            @pl.when(g + 2 * LEAD < groups)
            def _():
                start_kv(g + 2 * LEAD)

    others = ((0, 4), (1, 2), (3, 5))

    def gradients(g, first, second):
        stat_wait(xr1, recv_x1.at[g], g)
        factors, deltas = [], []
        for n in range(3):
            stats = [xs1[g, n], xr1[g, others[n][0]], xr1[g, others[n][1]]]
            top = jnp.maximum(
                jnp.maximum(stats[0][:GROUP], stats[1][:GROUP]), stats[2][:GROUP]
            )
            shares = [jnp.exp2(stat[:GROUP] - top) for stat in stats]
            inverse = 1.0 / (shares[0] + shares[1] + shares[2])
            delta = sum(share * stat[GROUP:] for share, stat in zip(shares, stats))
            factors.append(jnp.exp2(tops[g, n, pl.ds(0, GROUP)] - top) * inverse)
            deltas.append(delta * inverse)
        pairs = []
        for i in range(GROUP):
            h = g * GROUP + i
            lows, scores = [], []
            for n, at in enumerate(slots):
                probs = weights[h, :, at] * factors[n][i:i + 1]
                lows.append(probs.astype(bf16))
                scores.append((probs * (grads[h, :, at] - deltas[n][i:i + 1]) * inv_root).astype(bf16))
            low = jnp.concatenate(lows, axis=1)
            score = jnp.concatenate(scores, axis=1)
            pairs.append((h, low, score))
            grad_query = dot(score, kv[0, h], tn)
            dq_send[0, h] = grad_query[:128].astype(bf16)
            dq_own[h] = grad_query[128:256]
            dq_send[1, h] = grad_query[256:].astype(bf16)

        issue(first)
        issue(second)
        for h, low, score in pairs:
            grad_value = dot(low, gb[h], nn)
            dv_own[h] = grad_value[:128]
            dkv_send[0, 1, h] = grad_value[128:192].astype(bf16)
            dkv_send[1, 1, h] = grad_value[192:].astype(bf16)
            grad_key = dot(score, qb[h], nn)
            dk_own[h] = grad_key[:128]
            dkv_send[0, 0, h] = grad_key[128:192].astype(bf16)
            dkv_send[1, 0, h] = grad_key[192:].astype(bf16)

        start_grad(g)

        @pl.when(g > 0)
        def _():
            forward_grad(g - 1)

    @pl.loop(0, len(STEPS))
    def _(t):
        stage, g, first, second = (
            sum((t == n).astype(jnp.int32) * step[at] for n, step in enumerate(STEPS))
            for at in range(4)
        )
        for n, run in enumerate((exponents, gradients)):
            @pl.when(stage == n)
            def _(run=run):
                run(g, first, second)

    def fold(own, n, h):
        blocks = own[h].reshape(8, 2, 8, LANES)
        sides = [dkv_recv[side, n, h].astype(f32).reshape(8, 1, 8, LANES) for side in range(2)]
        return (blocks + jnp.concatenate(sides, axis=1)).reshape(128, LANES).astype(bf16)

    def finish_keys(g):
        wait_halos(dkv_recv, recv_dkv.at[g], pl.ds(g * GROUP, GROUP))
        for i in range(GROUP):
            h = g * GROUP + i
            ok_ref[:, head_cols(h)] = fold(dk_own, 0, h)
            ov_ref[:, head_cols(h)] = fold(dv_own, 1, h)

    def finish_queries(g):
        heads = pl.ds(g * GROUP, GROUP)
        wait_two(dq_recv, recv_dq.at[g], heads, has_up, has_down)
        for i in range(GROUP):
            h = g * GROUP + i
            oq_ref[:, head_cols(h)] = (
                dq_own[h] + dq_recv[0, h].astype(f32) + dq_recv[1, h].astype(f32)
            ).astype(bf16)

    @pl.loop(0, groups)
    def _(g):
        finish_keys(g)
        finish_queries(g)

    @pl.when(sec > 0)
    def _():
        sec_copy.wait_send()

    every = pl.ds(0, HEADS)
    wait_pair(has_up, has_down, bias.at[pl.ds(0, 2)], bias.at[0], bias_sem.at[0])
    wait_rows(qb, send_q.at[0], every)
    wait_rows(gb, send_g.at[0], every)
    wait_two(dq_send, send_dq.at[0], every, has_up, has_down)
    stat_wait(xr1, send_x1.at[0], pl.ds(0, groups))
    wait_halos(kv_send, send_kv.at[0], every)
    wait_halos(dkv_send, send_dkv.at[0], every)
    if detour:
        for n, (names, buf) in enumerate(((VIA_KV, via_kv), (VIA_GRAD, via_dkv))):
            @pl.when(via_holder(0) | via_holder(1))
            def _(n=n, names=names, buf=buf):
                ref = buf.at[:, pl.ds(0, GROUP * len(names))]
                pltpu.make_async_copy(ref, ref, send_via.at[n]).wait()


def store_kernel(aq, ak, av, oq, ok, ov, sems):
    stores = [
        pltpu.make_async_copy(src, dst, sems.at[n])
        for n, (src, dst) in enumerate(((aq, oq), (ak, ok), (av, ov)))
    ]
    for store in stores:
        store.start()
    for store in stores:
        store.wait()


def relay_body(queries, keys, values, cotangent, upstream, block_mask):
    sections, rows_n, cols_n = (lax.axis_size(a) for a in ("section", "ha", "wa"))
    shape = queries.shape
    tokens = shape[1] * shape[2] * shape[3]
    flat = (tokens, shape[4])
    groups = HEADS // GROUP
    bf16, f32 = jnp.bfloat16, jnp.float32
    dma = pltpu.SemaphoreType.DMA
    vmem = pltpu.VMEM
    out = pl.pallas_call(
        functools.partial(relay_kernel, sections, rows_n, cols_n),
        out_shape=[vmem(flat, bf16)] * 3,
        in_specs=[pl.BlockSpec(memory_space=pltpu.HBM)] * 6,
        out_specs=[pl.BlockSpec(memory_space=pltpu.VMEM)] * 3,
        scratch_shapes=[
            vmem(flat, bf16), vmem(flat, bf16), vmem(flat, bf16), vmem(flat, bf16),
            pltpu.SMEM((2, 9), jnp.int32),
            vmem(flat, bf16),
            vmem((HEADS, 384, LANES), bf16), vmem((HEADS, 384, LANES), bf16),
            vmem((2, HEADS, 256, LANES), bf16), vmem((2, 2, HEADS, 64, LANES), bf16),
            vmem((3, 4, LANES), f32), vmem((3, 4, LANES), f32), vmem((3, 4, 8, LANES), f32),
            vmem((HEADS, 256, 384), f32), vmem((HEADS, 256, 384), f32),
            vmem((groups, 3, 8, LANES), f32),
            vmem((groups, 3, 2 * GROUP, LANES), f32), vmem((groups, 6, 2 * GROUP, LANES), f32),
            vmem((HEADS, 128, LANES), f32),
            vmem((2, HEADS, 128, LANES), bf16), vmem((2, HEADS, 128, LANES), bf16),
            vmem((HEADS, 128, LANES), f32), vmem((HEADS, 128, LANES), f32),
            vmem((2, 2, HEADS, 64, LANES), bf16), vmem((2, 2, HEADS, 64, LANES), bf16),
            vmem((2, HEADS, 64, LANES), bf16), vmem((2, HEADS, 64, LANES), bf16),
            dma((6,)), dma((2,)), dma((2,)),
            dma((1,)), dma((1,)), dma((1,)), dma((1,)), dma((1,)), dma((1,)), dma((2,)),
            dma((groups,)), dma((groups,)), dma((groups,)), dma((groups,)), dma((groups,)),
            dma((2, groups)),
        ],
        compiler_params=pltpu.CompilerParams(
            collective_id=0, has_side_effects=True, vmem_limit_bytes=61 * 2**20
        ),
    )(
        queries.reshape(flat), keys.reshape(flat), values.reshape(flat),
        cotangent.reshape(flat), upstream.reshape(flat), block_mask.reshape(2, 9),
    )
    out = pl.pallas_call(
        store_kernel,
        out_shape=[jax.ShapeDtypeStruct(flat, bf16)] * 3,
        in_specs=[pl.BlockSpec(memory_space=pltpu.VMEM)] * 3,
        out_specs=[pl.BlockSpec(memory_space=pltpu.HBM)] * 3,
        scratch_shapes=[dma((3,))],
        compiler_params=pltpu.CompilerParams(vmem_limit_bytes=4 * 2**20),
    )(*out)
    return tuple(x.reshape(shape) for x in out)


def solution(mesh):
    return jax.shard_map(
        relay_body,
        mesh=mesh,
        in_specs=(
            P("section", None, "ha", "wa", None),
            P("section", None, "ha", "wa", None),
            P("section", None, "ha", "wa", None),
            P("section", None, "ha", "wa", None),
            P("section", None, "ha", "wa", None),
            P("section", "ha", "wa", None),
        ),
        out_specs=(
            P("section", None, "ha", "wa", None),
            P("section", None, "ha", "wa", None),
            P("section", None, "ha", "wa", None),
        ),
        check_vma=False,
    )
```

```python
import functools

import jax
import jax.numpy as jnp
from jax import lax
from jax.experimental import pallas as pl
from jax.experimental.pallas import tpu as pltpu
from jax.sharding import PartitionSpec as P

HEADS = 12
HEAD_DIM = 128
TILE = 8


NEG = -1e30
LANES = 128
GROUP = 2
LEAD = 3
FIRST = (0, 1)
SECOND = (6, 2, 7, 8)
STEPS = (
    (0, 0, 3, 9), (0, 1, 10, -1), (0, 2, 4, 5), (1, 0, 11, -1), (0, 3, -1, -1), (1, 1, 12, -1),
    (0, 4, -1, -1), (1, 2, 13, -1), (0, 5, 14, -1), (1, 3, 15, -1), (1, 4, 16, -1), (1, 5, 17, -1),
)
VIA_KV = (1, 3, 5)
VIA_GRAD = (0, 2, 4)
MESH_ID = pl.DeviceIdType.MESH


def relay_kernel(
    sections, rows_n, cols_n,
    q_hbm, k_hbm, v_hbm, c_hbm, u_hbm, mask_hbm,
    oq_ref, ok_ref, ov_ref,
    q_ref, k_ref, v_ref, c_ref, mask_ref, handed,
    qb, gb, kv, kv_send, bias_send, bias, bias_tiles,
    weights, grads, tops, xs1, xr1,
    dq_own, dq_send, dq_recv, dk_own, dv_own, dkv_send, dkv_recv, via_kv, via_dkv,
    load_sem, sec_sem, bias_sem, send_q, send_g, send_dq, send_kv, send_dkv, send_x1, send_via,
    recv_q, recv_dq, recv_kv, recv_dkv, recv_x1, recv_via,
):
    f32, bf16 = jnp.float32, jnp.bfloat16
    sec = lax.axis_index("section")
    row = lax.axis_index("ha")
    col = lax.axis_index("wa")
    groups = HEADS // GROUP
    inv_root = HEAD_DIM ** (-0.5)
    scale = inv_root * 1.4426950408889634
    has_up, has_down = row > 0, row < rows_n - 1
    has_up2, has_down2 = row > 1, row < rows_n - 2
    has_left, has_right = col > 0, col < cols_n - 1
    detour = cols_n == 4

    ahead, rest = pl.ds(0, GROUP * LANES), pl.ds(GROUP * LANES, (HEADS - GROUP) * LANES)
    loads = [
        pltpu.make_async_copy(src, dst, load_sem.at[n])
        for n, (src, dst) in enumerate(
            (
                (q_hbm.at[:, ahead], q_ref.at[:, ahead]), (k_hbm, k_ref), (v_hbm, v_ref),
                (mask_hbm, mask_ref), (c_hbm, c_ref), (q_hbm.at[:, rest], q_ref.at[:, rest]),
            )
        )
    ]
    for n in (0, 5, 1, 2, 3, 4):
        loads[n].start()

    barrier = pltpu.get_barrier_semaphore()
    greeted = [
        (has_up, {"ha": row - 1}),
        (has_down, {"ha": row + 1}),
        (has_up2, {"ha": row - 2}),
        (has_down2, {"ha": row + 2}),
        (has_left, {"wa": col - 1}),
        (has_right, {"wa": col + 1}),
        (sec > 0, {"section": sec - 1}),
        (sec < sections - 1, {"section": sec + 1}),
    ]
    if detour:
        greeted.append((col >= 0, {"wa": lax.rem(col + 2, 4)}))
    expected = jnp.int32(0)
    for cond, dev in greeted:
        @pl.when(cond)
        def _(dev=dev):
            pl.semaphore_signal(barrier, inc=1, device_id=dev, device_id_type=MESH_ID)

        expected = expected + cond.astype(jnp.int32)

    def remote(src, dst, send, recv, dev):
        return pltpu.make_async_remote_copy(
            src_ref=src, dst_ref=dst, send_sem=send, recv_sem=recv,
            device_id=dev, device_id_type=MESH_ID,
        )

    vertical = ((has_up, has_down, {"ha": row - 1}), (has_down, has_up, {"ha": row + 1}))
    sideways = ((has_left, has_right, {"wa": col - 1}), (has_right, has_left, {"wa": col + 1}))

    def slot_rows(d):
        return pl.ds(256 - 256 * d, 128)

    def halo_rows(side):
        return pl.ds(192 - 64 * side, 64)

    sec_copy = remote(u_hbm, handed, sec_sem.at[0], sec_sem.at[1], {"section": sec - 1})

    def bias_copy(d):
        return remote(
            bias_send.at[2 * d], bias.at[2 - 2 * d], bias_sem.at[0], bias_sem.at[1],
            vertical[d][2],
        )

    def rows_copy(buf, send, recv, d, heads, g):
        return remote(
            buf.at[heads, pl.ds(128, 128)], buf.at[heads, slot_rows(d)],
            send.at[0], recv.at[g], vertical[d][2],
        )

    def q_copy(d, g):
        return rows_copy(qb, send_q, recv_q, d, pl.ds(g * GROUP, GROUP), g)

    def g_copy(d, g):
        return rows_copy(gb, send_g, recv_q, d, pl.ds(g * GROUP, GROUP), g)

    def dq_copy(d, g):
        heads = pl.ds(g * GROUP, GROUP)
        return remote(
            dq_send.at[d, heads], dq_recv.at[1 - d, heads],
            send_dq.at[0], recv_dq.at[g], vertical[d][2],
        )

    def kv_copy(side, g):
        heads = pl.ds(g * GROUP, GROUP)
        return remote(
            kv_send.at[side, :, heads], kv.at[:, heads, halo_rows(side)],
            send_kv.at[0], recv_kv.at[g], sideways[side][2],
        )

    def grad_copy(side, g):
        heads = pl.ds(g * GROUP, GROUP)
        return remote(
            dkv_send.at[side, :, heads], dkv_recv.at[1 - side, :, heads],
            send_dkv.at[0], recv_dkv.at[g], sideways[side][2],
        )

    def via_source(side):
        return col == (2, 1)[side]

    def via_holder(side):
        return col == (0, 3)[side]

    def via_kv_in(side, g):
        heads = pl.ds(g * GROUP, GROUP)
        return remote(
            kv_send.at[side, :, heads], via_kv.at[:, heads], send_kv.at[0], recv_via.at[0, g],
            {"wa": jnp.int32((0, 3)[side])},
        )

    def via_kv_out(side, g):
        heads = pl.ds(g * GROUP, GROUP)
        return remote(
            via_kv.at[:, heads], kv.at[:, heads, halo_rows(side)], send_via.at[0], recv_kv.at[g],
            {"wa": jnp.int32((1, 2)[side])},
        )

    def via_grad_in(side, g):
        heads = pl.ds(g * GROUP, GROUP)
        return remote(
            dkv_send.at[side, :, heads], via_dkv.at[:, heads], send_dkv.at[0], recv_via.at[1, g],
            {"wa": jnp.int32((0, 3)[side])},
        )

    def via_grad_out(side, g):
        heads = pl.ds(g * GROUP, GROUP)
        return remote(
            via_dkv.at[:, heads], dkv_recv.at[1 - side, :, heads], send_via.at[1], recv_dkv.at[g],
            {"wa": jnp.int32((1, 2)[side])},
        )

    def is_in(g, names):
        return sum((g == n).astype(jnp.int32) for n in names) > 0

    def start_side(names, copy, inward, g):
        g = jnp.int32(g)
        for side in range(2):
            if detour:
                around = via_source(side) & is_in(g, names)

                @pl.when(around)
                def _(side=side):
                    inward(side, g).start()

                @pl.when(sideways[side][0] & ~around)
                def _(side=side):
                    copy(side, g).start()
            else:
                @pl.when(sideways[side][0])
                def _(side=side):
                    copy(side, g).start()

    def forward(names, inward, outward, g):
        g = jnp.int32(g)
        if detour:
            for side in range(2):
                @pl.when(via_holder(side) & is_in(g, names))
                def _(side=side):
                    inward(side, g).wait_recv()
                    outward(side, g).start()

    def start_kv(g):
        start_side(VIA_KV, kv_copy, via_kv_in, g)

    def start_grad(g):
        start_side(VIA_GRAD, grad_copy, via_grad_in, g)

    def forward_kv(g):
        forward(VIA_KV, via_kv_in, via_kv_out, g)

    def forward_grad(g):
        forward(VIA_GRAD, via_grad_in, via_grad_out, g)

    stat_moves = (
        (has_up, has_down, {"ha": row - 1}, pl.ds(0, 2), pl.ds(2, 2)),
        (has_down, has_up, {"ha": row + 1}, pl.ds(1, 2), pl.ds(0, 2)),
        (has_up2, has_down2, {"ha": row - 2}, pl.ds(0, 1), pl.ds(5, 1)),
        (has_down2, has_up2, {"ha": row + 2}, pl.ds(2, 1), pl.ds(4, 1)),
    )

    def stat_copy(xs, xr, send, recv, m, g):
        _, _, dev, mine, theirs = stat_moves[m]
        return remote(xs.at[g, mine], xr.at[g, theirs], send.at[0], recv.at[g], dev)

    def stat_start(xs, xr, send, recv, g):
        for m in range(4):
            @pl.when(stat_moves[m][0])
            def _(m=m):
                stat_copy(xs, xr, send, recv, m, g).start()

    def stat_tiles(at):
        return 2 * ((at > 0) + (at < rows_n - 1)) + (at > 1) + (at < rows_n - 2)

    tiles_here = sum(
        n * cond.astype(jnp.int32)
        for n, cond in ((2, has_up), (2, has_down), (1, has_up2), (1, has_down2))
    )

    def stat_wait(xr, sem, g):
        for tiles in sorted({stat_tiles(at) for at in range(rows_n)} - {0}):
            @pl.when(tiles_here == tiles)
            def _(tiles=tiles):
                ref = xr.at[g, pl.ds(0, tiles)]
                pltpu.make_async_copy(ref, ref, sem).wait()

    def wait_pair(first, second, ref_both, ref_one, sem):
        @pl.when(first & second)
        def _():
            pltpu.make_async_copy(ref_both, ref_both, sem).wait()

        @pl.when(first ^ second)
        def _():
            pltpu.make_async_copy(ref_one, ref_one, sem).wait()

    def wait_rows(buf, sem, heads):
        wait_pair(
            has_up, has_down, buf.at[heads, pl.ds(0, 256)], buf.at[heads, pl.ds(0, 128)], sem
        )

    def wait_halos(buf, sem, heads):
        wait_pair(has_left, has_right, buf.at[:, :, heads], buf.at[0, :, heads], sem)

    def wait_two(buf, sem, heads, first, second):
        wait_pair(first, second, buf.at[:, heads], buf.at[0, heads], sem)

    def issue(chunk):
        kind, g = lax.div(chunk, groups), lax.rem(chunk, groups)

        @pl.when(chunk >= 0)
        def _():
            for n, copy in enumerate((q_copy, g_copy, dq_copy)):
                @pl.when(kind == n)
                def _(copy=copy):
                    for d in range(2):
                        @pl.when(vertical[d][0])
                        def _(d=d):
                            copy(d, g).start()

    def head_cols(head):
        return pl.ds(pl.multiple_of(head * LANES, LANES), LANES)

    def split(block):
        tiles = block.astype(f32).reshape(8, 2, 8, LANES)
        return [tiles[:, t].reshape(64, LANES).astype(bf16) for t in range(2)]

    def spread(ref, n):
        @pl.loop(0, HEADS)
        def _(h):
            block = ref[:, head_cols(h)]
            kv[n, h, pl.ds(0, 128)] = block
            for side, part in enumerate(split(block)):
                kv_send[side, n, h] = part

    loads[0].wait()

    def place_q(h):
        qb[h, pl.ds(128, 128)] = q_ref[:, head_cols(h)]

    for h in range(GROUP):
        place_q(h)

    pl.semaphore_wait(barrier, expected)

    issue(jnp.int32(FIRST[0]))
    loads[5].wait()
    pl.loop(GROUP, HEADS)(place_q)

    @pl.when(sec > 0)
    def _():
        sec_copy.start()

    for chunk in FIRST[1:]:
        issue(jnp.int32(chunk))

    loads[1].wait()
    spread(k_ref, 0)
    loads[2].wait()
    spread(v_ref, 1)
    for g in range(LEAD):
        start_kv(g)


    loads[3].wait()
    lane = lax.broadcasted_iota(jnp.int32, (1, LANES), 1)
    first_tile = lax.rem(lane // TILE, 2) == 0
    dead = jnp.int32(0)
    left = jnp.where(has_left, 1, 0)
    right = jnp.where(has_right, 1, 0)
    for i in range(3):
        entry = [[mask_ref[t, 3 * i + j] for j in range(3)] for t in range(2)]
        for n, (first, second) in enumerate((
            (entry[0][1], entry[1][0]),
            (entry[0][2], entry[1][1]),
            (entry[0][0] * left, dead),
            (dead, entry[1][2] * right),
        )):
            seen = jnp.where(first_tile, first, second)
            bias_send[i, pl.ds(n, 1)] = jnp.where(seen > 0, 0.0, NEG).astype(f32)
    bias[1] = bias_send[1]

    for d in range(2):
        @pl.when(vertical[d][0])
        def _(d=d):
            bias_copy(d).start()


    for cond, at in ((row == 0, 0), (row == rows_n - 1, 256)):
        @pl.when(cond)
        def _(at=at):
            bias[2 * at // 256] = jnp.zeros((4, LANES), f32)

            @pl.loop(0, HEADS)
            def _(h):
                qb[h, pl.ds(at, 128)] = jnp.zeros((128, LANES), bf16)
                gb[h, pl.ds(at, 128)] = jnp.zeros((128, LANES), bf16)
                dq_recv[at // 256, h] = jnp.zeros((128, LANES), bf16)

    for cond, side in ((col == 0, 0), (col == cols_n - 1, 1)):
        @pl.when(cond)
        def _(side=side):
            @pl.loop(0, HEADS)
            def _(h):
                for n in range(2):
                    kv[n, h, pl.ds(128 + 64 * side, 64)] = jnp.zeros((64, LANES), bf16)
                    dkv_recv[side, n, h] = jnp.zeros((64, LANES), bf16)

    stat_row = lax.broadcasted_iota(jnp.int32, (2 * GROUP, LANES), 0)
    no_stat = jnp.where(stat_row < GROUP, NEG, 0.0).astype(f32)
    for cond, pieces in (
        (row == 0, (0, 1)), (row < 2, (4,)),
        (row == rows_n - 1, (2, 3)), (row > rows_n - 3, (5,)),
    ):
        @pl.when(cond)
        def _(pieces=pieces):
            for g in range(groups):
                for piece in pieces:
                    xr1[g, piece] = no_stat

    @pl.when(sec == sections - 1)
    def _():
        handed[...] = jnp.zeros_like(handed)

    @pl.when(sec < sections - 1)
    def _():
        sec_copy.wait_recv()

    loads[4].wait()

    @pl.loop(0, HEADS)
    def _(h):
        at = head_cols(h)
        gb[h, pl.ds(128, 128)] = (c_ref[:, at].astype(f32) + handed[:, at].astype(f32)).astype(bf16)

    for chunk in SECOND:
        issue(jnp.int32(chunk))

    for g in range(LEAD):
        forward_kv(g)
        start_kv(g + LEAD)

    wait_pair(has_up, has_down, bias.at[pl.ds(0, 2)], bias.at[0], bias_sem.at[1])
    for n in range(3):
        for k in range(4):
            bias_tiles[n, k] = jnp.broadcast_to(bias[n, pl.ds(k, 1)], (8, LANES))

    nt = (((1,), (1,)), ((), ()))
    nn = (((1,), (0,)), ((), ()))
    tn = (((0,), (0,)), ((), ()))

    def dot(a, b, dims):
        return lax.dot_general(a, b, dims, preferred_element_type=f32)

    slots = [slice(n * 128, n * 128 + 128) for n in range(3)]

    def exponents(g, first, second):
        heads = pl.ds(g * GROUP, GROUP)
        wait_rows(qb, recv_q.at[g], pl.ds(0, 2 * GROUP))
        wait_halos(kv_send, recv_kv.at[g], heads)
        for i in range(GROUP):
            h = g * GROUP + i
            part = dot(kv[0, h], qb[h], nt)
            grad_part = dot(kv[1, h], gb[h], nt)
            for n, at in enumerate(slots):
                rows = part[:, at] * scale
                scores = jnp.concatenate(
                    [
                        (rows[:128].reshape(8, 2, 8, LANES) + bias_tiles[n, 0:2][None]).reshape(128, LANES),
                        (rows[128:192].reshape(8, 8, LANES) + bias_tiles[n, 2][None]).reshape(64, LANES),
                        (rows[192:].reshape(8, 8, LANES) + bias_tiles[n, 3][None]).reshape(64, LANES),
                    ],
                    axis=0,
                )
                top = jnp.max(scores, axis=0, keepdims=True)
                exps = jnp.exp2(scores - top)
                weights[h, :, at] = exps
                grads[h, :, at] = grad_part[:, at]
                total = jnp.sum(exps, axis=0, keepdims=True)
                delta = jnp.sum(exps * grad_part[:, at], axis=0, keepdims=True)
                tops[g, n, pl.ds(i, 1)] = top
                xs1[g, n, pl.ds(i, 1)] = top + jnp.log(total) * 1.4426950408889634
                xs1[g, n, pl.ds(GROUP + i, 1)] = delta / total

        stat_start(xs1, xr1, send_x1, recv_x1, g)
        issue(first)
        issue(second)

        @pl.when(g + LEAD < groups)
        def _():
            forward_kv(g + LEAD)

            @pl.when(g + 2 * LEAD < groups)
            def _():
                start_kv(g + 2 * LEAD)

    others = ((0, 4), (1, 2), (3, 5))

    def gradients(g, first, second):
        stat_wait(xr1, recv_x1.at[g], g)
        factors, deltas = [], []
        for n in range(3):
            stats = [xs1[g, n], xr1[g, others[n][0]], xr1[g, others[n][1]]]
            top = jnp.maximum(
                jnp.maximum(stats[0][:GROUP], stats[1][:GROUP]), stats[2][:GROUP]
            )
            shares = [jnp.exp2(stat[:GROUP] - top) for stat in stats]
            inverse = 1.0 / (shares[0] + shares[1] + shares[2])
            delta = sum(share * stat[GROUP:] for share, stat in zip(shares, stats))
            factors.append(jnp.exp2(tops[g, n, pl.ds(0, GROUP)] - top) * inverse)
            deltas.append(delta * inverse)
        pairs = []
        for i in range(GROUP):
            h = g * GROUP + i
            lows, scores = [], []
            for n, at in enumerate(slots):
                probs = weights[h, :, at] * factors[n][i:i + 1]
                lows.append(probs.astype(bf16))
                scores.append((probs * (grads[h, :, at] - deltas[n][i:i + 1]) * inv_root).astype(bf16))
            low = jnp.concatenate(lows, axis=1)
            score = jnp.concatenate(scores, axis=1)
            pairs.append((h, low, score))
            grad_query = dot(score, kv[0, h], tn)
            dq_send[0, h] = grad_query[:128].astype(bf16)
            dq_own[h] = grad_query[128:256]
            dq_send[1, h] = grad_query[256:].astype(bf16)

        issue(first)
        issue(second)
        for h, low, score in pairs:
            grad_value = dot(low, gb[h], nn)
            dv_own[h] = grad_value[:128]
            dkv_send[0, 1, h] = grad_value[128:192].astype(bf16)
            dkv_send[1, 1, h] = grad_value[192:].astype(bf16)
            grad_key = dot(score, qb[h], nn)
            dk_own[h] = grad_key[:128]
            dkv_send[0, 0, h] = grad_key[128:192].astype(bf16)
            dkv_send[1, 0, h] = grad_key[192:].astype(bf16)

        start_grad(g)

        @pl.when(g > 0)
        def _():
            forward_grad(g - 1)

    @pl.loop(0, len(STEPS))
    def _(t):
        stage, g, first, second = (
            sum((t == n).astype(jnp.int32) * step[at] for n, step in enumerate(STEPS))
            for at in range(4)
        )
        for n, run in enumerate((exponents, gradients)):
            @pl.when(stage == n)
            def _(run=run):
                run(g, first, second)

    def fold(own, n, h):
        blocks = own[h].reshape(8, 2, 8, LANES)
        sides = [dkv_recv[side, n, h].astype(f32).reshape(8, 1, 8, LANES) for side in range(2)]
        return (blocks + jnp.concatenate(sides, axis=1)).reshape(128, LANES).astype(bf16)

    def finish_keys(g):
        wait_halos(dkv_recv, recv_dkv.at[g], pl.ds(g * GROUP, GROUP))
        for i in range(GROUP):
            h = g * GROUP + i
            ok_ref[:, head_cols(h)] = fold(dk_own, 0, h)
            ov_ref[:, head_cols(h)] = fold(dv_own, 1, h)

    def finish_queries(g):
        heads = pl.ds(g * GROUP, GROUP)
        wait_two(dq_recv, recv_dq.at[g], heads, has_up, has_down)
        for i in range(GROUP):
            h = g * GROUP + i
            oq_ref[:, head_cols(h)] = (
                dq_own[h] + dq_recv[0, h].astype(f32) + dq_recv[1, h].astype(f32)
            ).astype(bf16)

    @pl.loop(0, groups)
    def _(g):
        finish_keys(g)
        finish_queries(g)

    @pl.when(sec > 0)
    def _():
        sec_copy.wait_send()

    every = pl.ds(0, HEADS)
    wait_pair(has_up, has_down, bias.at[pl.ds(0, 2)], bias.at[0], bias_sem.at[0])
    wait_rows(qb, send_q.at[0], every)
    wait_rows(gb, send_g.at[0], every)
    wait_two(dq_send, send_dq.at[0], every, has_up, has_down)
    stat_wait(xr1, send_x1.at[0], pl.ds(0, groups))
    wait_halos(kv_send, send_kv.at[0], every)
    wait_halos(dkv_send, send_dkv.at[0], every)
    if detour:
        for n, (names, buf) in enumerate(((VIA_KV, via_kv), (VIA_GRAD, via_dkv))):
            @pl.when(via_holder(0) | via_holder(1))
            def _(n=n, names=names, buf=buf):
                ref = buf.at[:, pl.ds(0, GROUP * len(names))]
                pltpu.make_async_copy(ref, ref, send_via.at[n]).wait()


def store_kernel(aq, ak, av, oq, ok, ov, sems):
    stores = [
        pltpu.make_async_copy(src, dst, sems.at[n])
        for n, (src, dst) in enumerate(((aq, oq), (ak, ok), (av, ov)))
    ]
    for store in stores:
        store.start()
    for store in stores:
        store.wait()


def relay_body(queries, keys, values, cotangent, upstream, block_mask):
    sections, rows_n, cols_n = (lax.axis_size(a) for a in ("section", "ha", "wa"))
    shape = queries.shape
    tokens = shape[1] * shape[2] * shape[3]
    flat = (tokens, shape[4])
    groups = HEADS // GROUP
    bf16, f32 = jnp.bfloat16, jnp.float32
    dma = pltpu.SemaphoreType.DMA
    vmem = pltpu.VMEM
    out = pl.pallas_call(
        functools.partial(relay_kernel, sections, rows_n, cols_n),
        out_shape=[vmem(flat, bf16)] * 3,
        in_specs=[pl.BlockSpec(memory_space=pltpu.HBM)] * 6,
        out_specs=[pl.BlockSpec(memory_space=pltpu.VMEM)] * 3,
        scratch_shapes=[
            vmem(flat, bf16), vmem(flat, bf16), vmem(flat, bf16), vmem(flat, bf16),
            pltpu.SMEM((2, 9), jnp.int32),
            vmem(flat, bf16),
            vmem((HEADS, 384, LANES), bf16), vmem((HEADS, 384, LANES), bf16),
            vmem((2, HEADS, 256, LANES), bf16), vmem((2, 2, HEADS, 64, LANES), bf16),
            vmem((3, 4, LANES), f32), vmem((3, 4, LANES), f32), vmem((3, 4, 8, LANES), f32),
            vmem((HEADS, 256, 384), f32), vmem((HEADS, 256, 384), f32),
            vmem((groups, 3, 8, LANES), f32),
            vmem((groups, 3, 2 * GROUP, LANES), f32), vmem((groups, 6, 2 * GROUP, LANES), f32),
            vmem((HEADS, 128, LANES), f32),
            vmem((2, HEADS, 128, LANES), bf16), vmem((2, HEADS, 128, LANES), bf16),
            vmem((HEADS, 128, LANES), f32), vmem((HEADS, 128, LANES), f32),
            vmem((2, 2, HEADS, 64, LANES), bf16), vmem((2, 2, HEADS, 64, LANES), bf16),
            vmem((2, HEADS, 64, LANES), bf16), vmem((2, HEADS, 64, LANES), bf16),
            dma((6,)), dma((2,)), dma((2,)),
            dma((1,)), dma((1,)), dma((1,)), dma((1,)), dma((1,)), dma((1,)), dma((2,)),
            dma((groups,)), dma((groups,)), dma((groups,)), dma((groups,)), dma((groups,)),
            dma((2, groups)),
        ],
        compiler_params=pltpu.CompilerParams(
            collective_id=0, has_side_effects=True, vmem_limit_bytes=61 * 2**20
        ),
    )(
        queries.reshape(flat), keys.reshape(flat), values.reshape(flat),
        cotangent.reshape(flat), upstream.reshape(flat), block_mask.reshape(2, 9),
    )
    out = pl.pallas_call(
        store_kernel,
        out_shape=[jax.ShapeDtypeStruct(flat, bf16)] * 3,
        in_specs=[pl.BlockSpec(memory_space=pltpu.VMEM)] * 3,
        out_specs=[pl.BlockSpec(memory_space=pltpu.HBM)] * 3,
        scratch_shapes=[dma((3,))],
        compiler_params=pltpu.CompilerParams(vmem_limit_bytes=4 * 2**20),
    )(*out)
    return tuple(x.reshape(shape) for x in out)


def solution(mesh):
    return jax.shard_map(
        relay_body,
        mesh=mesh,
        in_specs=(
            P("section", None, "ha", "wa", None),
            P("section", None, "ha", "wa", None),
            P("section", None, "ha", "wa", None),
            P("section", None, "ha", "wa", None),
            P("section", None, "ha", "wa", None),
            P("section", "ha", "wa", None),
        ),
        out_specs=(
            P("section", None, "ha", "wa", None),
            P("section", None, "ha", "wa", None),
            P("section", None, "ha", "wa", None),
        ),
        check_vma=False,
    )
```

```python
import functools

import jax
import jax.numpy as jnp
from jax import lax
from jax.experimental import pallas as pl
from jax.experimental.pallas import tpu as pltpu
from jax.sharding import PartitionSpec as P

HEADS = 12
HEAD_DIM = 128
TILE = 8


NEG = -1e30
LANES = 128
GROUP = 2
LEAD = 3
FIRST = (0, 1, 2)
SECOND = (6, 7, 8)
STEPS = (
    (0, 0, 3, 9), (0, 1, 10, -1), (0, 2, 4, 5), (1, 0, 11, -1), (0, 3, -1, -1), (1, 1, 12, -1),
    (0, 4, -1, -1), (1, 2, 13, -1), (0, 5, 14, -1), (1, 3, 15, -1), (1, 4, 16, -1), (1, 5, 17, -1),
)
VIA_KV = (1, 3, 5)
VIA_GRAD = (0, 2, 4)
MESH_ID = pl.DeviceIdType.MESH


def relay_kernel(
    sections, rows_n, cols_n,
    q_hbm, k_hbm, v_hbm, c_hbm, u_hbm, mask_hbm,
    oq_ref, ok_ref, ov_ref,
    q_ref, k_ref, v_ref, c_ref, mask_ref, handed,
    qb, gb, kv, kv_send, bias_send, bias, bias_tiles,
    weights, grads, tops, xs1, xr1,
    dq_own, dq_send, dq_recv, dk_own, dv_own, dkv_send, dkv_recv, via_kv, via_dkv,
    load_sem, sec_sem, bias_sem, send_q, send_g, send_dq, send_kv, send_dkv, send_x1, send_via,
    recv_q, recv_dq, recv_kv, recv_dkv, recv_x1, recv_via,
):
    f32, bf16 = jnp.float32, jnp.bfloat16
    sec = lax.axis_index("section")
    row = lax.axis_index("ha")
    col = lax.axis_index("wa")
    groups = HEADS // GROUP
    inv_root = HEAD_DIM ** (-0.5)
    scale = inv_root * 1.4426950408889634
    has_up, has_down = row > 0, row < rows_n - 1
    has_up2, has_down2 = row > 1, row < rows_n - 2
    has_left, has_right = col > 0, col < cols_n - 1
    detour = cols_n == 4

    ahead, rest = pl.ds(0, GROUP * LANES), pl.ds(GROUP * LANES, (HEADS - GROUP) * LANES)
    loads = [
        pltpu.make_async_copy(src, dst, load_sem.at[n])
        for n, (src, dst) in enumerate(
            (
                (q_hbm.at[:, ahead], q_ref.at[:, ahead]), (k_hbm, k_ref), (v_hbm, v_ref),
                (mask_hbm, mask_ref), (c_hbm, c_ref), (q_hbm.at[:, rest], q_ref.at[:, rest]),
            )
        )
    ]
    for n in (0, 5, 1, 2, 3, 4):
        loads[n].start()

    barrier = pltpu.get_barrier_semaphore()
    greeted = [
        (has_up, {"ha": row - 1}),
        (has_down, {"ha": row + 1}),
        (has_up2, {"ha": row - 2}),
        (has_down2, {"ha": row + 2}),
        (has_left, {"wa": col - 1}),
        (has_right, {"wa": col + 1}),
        (sec > 0, {"section": sec - 1}),
        (sec < sections - 1, {"section": sec + 1}),
    ]
    if detour:
        greeted.append((col >= 0, {"wa": lax.rem(col + 2, 4)}))
    expected = jnp.int32(0)
    for cond, dev in greeted:
        @pl.when(cond)
        def _(dev=dev):
            pl.semaphore_signal(barrier, inc=1, device_id=dev, device_id_type=MESH_ID)

        expected = expected + cond.astype(jnp.int32)

    def remote(src, dst, send, recv, dev):
        return pltpu.make_async_remote_copy(
            src_ref=src, dst_ref=dst, send_sem=send, recv_sem=recv,
            device_id=dev, device_id_type=MESH_ID,
        )

    vertical = ((has_up, has_down, {"ha": row - 1}), (has_down, has_up, {"ha": row + 1}))
    sideways = ((has_left, has_right, {"wa": col - 1}), (has_right, has_left, {"wa": col + 1}))

    def slot_rows(d):
        return pl.ds(256 - 256 * d, 128)

    def halo_rows(side):
        return pl.ds(192 - 64 * side, 64)

    sec_copy = remote(u_hbm, handed, sec_sem.at[0], sec_sem.at[1], {"section": sec - 1})

    def bias_copy(d):
        return remote(
            bias_send.at[2 * d], bias.at[2 - 2 * d], bias_sem.at[0], bias_sem.at[1],
            vertical[d][2],
        )

    def rows_copy(buf, send, recv, d, heads, g):
        return remote(
            buf.at[heads, pl.ds(128, 128)], buf.at[heads, slot_rows(d)],
            send.at[0], recv.at[g], vertical[d][2],
        )

    def q_copy(d, g):
        return rows_copy(qb, send_q, recv_q, d, pl.ds(g * GROUP, GROUP), g)

    def g_copy(d, g):
        return rows_copy(gb, send_g, recv_q, d, pl.ds(g * GROUP, GROUP), g)

    def dq_copy(d, g):
        heads = pl.ds(g * GROUP, GROUP)
        return remote(
            dq_send.at[d, heads], dq_recv.at[1 - d, heads],
            send_dq.at[0], recv_dq.at[g], vertical[d][2],
        )

    def kv_copy(side, g):
        heads = pl.ds(g * GROUP, GROUP)
        return remote(
            kv_send.at[side, :, heads], kv.at[:, heads, halo_rows(side)],
            send_kv.at[0], recv_kv.at[g], sideways[side][2],
        )

    def grad_copy(side, g):
        heads = pl.ds(g * GROUP, GROUP)
        return remote(
            dkv_send.at[side, :, heads], dkv_recv.at[1 - side, :, heads],
            send_dkv.at[0], recv_dkv.at[g], sideways[side][2],
        )

    def via_source(side):
        return col == (2, 1)[side]

    def via_holder(side):
        return col == (0, 3)[side]

    def via_kv_in(side, g):
        heads = pl.ds(g * GROUP, GROUP)
        return remote(
            kv_send.at[side, :, heads], via_kv.at[:, heads], send_kv.at[0], recv_via.at[0, lax.div(g, 2)],
            {"wa": jnp.int32((0, 3)[side])},
        )

    def via_kv_out(side, g):
        heads = pl.ds(g * GROUP, GROUP)
        return remote(
            via_kv.at[:, heads], kv.at[:, heads, halo_rows(side)], send_via.at[0], recv_kv.at[g],
            {"wa": jnp.int32((1, 2)[side])},
        )

    def via_grad_in(side, g):
        heads = pl.ds(g * GROUP, GROUP)
        return remote(
            dkv_send.at[side, :, heads], via_dkv.at[:, heads], send_dkv.at[0], recv_via.at[1, lax.div(g, 2)],
            {"wa": jnp.int32((0, 3)[side])},
        )

    def via_grad_out(side, g):
        heads = pl.ds(g * GROUP, GROUP)
        return remote(
            via_dkv.at[:, heads], dkv_recv.at[1 - side, :, heads], send_via.at[1], recv_dkv.at[g],
            {"wa": jnp.int32((1, 2)[side])},
        )

    def is_in(g, names):
        return sum((g == n).astype(jnp.int32) for n in names) > 0

    def start_side(names, copy, inward, g):
        g = jnp.int32(g)
        for side in range(2):
            if detour:
                around = via_source(side) & is_in(g, names)

                @pl.when(around)
                def _(side=side):
                    inward(side, g).start()

                @pl.when(sideways[side][0] & ~around)
                def _(side=side):
                    copy(side, g).start()
            else:
                @pl.when(sideways[side][0])
                def _(side=side):
                    copy(side, g).start()

    def forward(names, inward, outward, g):
        g = jnp.int32(g)
        if detour:
            for side in range(2):
                @pl.when(via_holder(side) & is_in(g, names))
                def _(side=side):
                    inward(side, g).wait_recv()
                    outward(side, g).start()

    def start_kv(g):
        start_side(VIA_KV, kv_copy, via_kv_in, g)

    def start_grad(g):
        start_side(VIA_GRAD, grad_copy, via_grad_in, g)

    def forward_kv(g):
        forward(VIA_KV, via_kv_in, via_kv_out, g)

    def forward_grad(g):
        forward(VIA_GRAD, via_grad_in, via_grad_out, g)

    stat_moves = (
        (has_up, has_down, {"ha": row - 1}, pl.ds(0, 2), pl.ds(2, 2)),
        (has_down, has_up, {"ha": row + 1}, pl.ds(1, 2), pl.ds(0, 2)),
        (has_up2, has_down2, {"ha": row - 2}, pl.ds(0, 1), pl.ds(5, 1)),
        (has_down2, has_up2, {"ha": row + 2}, pl.ds(2, 1), pl.ds(4, 1)),
    )

    def stat_copy(xs, xr, send, recv, m, g):
        _, _, dev, mine, theirs = stat_moves[m]
        return remote(xs.at[g, mine], xr.at[g, theirs], send.at[0], recv.at[g], dev)

    def stat_start(xs, xr, send, recv, g):
        for m in range(4):
            @pl.when(stat_moves[m][0])
            def _(m=m):
                stat_copy(xs, xr, send, recv, m, g).start()

    def stat_tiles(at):
        return 2 * ((at > 0) + (at < rows_n - 1)) + (at > 1) + (at < rows_n - 2)

    tiles_here = sum(
        n * cond.astype(jnp.int32)
        for n, cond in ((2, has_up), (2, has_down), (1, has_up2), (1, has_down2))
    )

    def stat_wait(xr, sem, g):
        for tiles in sorted({stat_tiles(at) for at in range(rows_n)} - {0}):
            @pl.when(tiles_here == tiles)
            def _(tiles=tiles):
                ref = xr.at[g, pl.ds(0, tiles)]
                pltpu.make_async_copy(ref, ref, sem).wait()

    def wait_pair(first, second, ref_both, ref_one, sem):
        @pl.when(first & second)
        def _():
            pltpu.make_async_copy(ref_both, ref_both, sem).wait()

        @pl.when(first ^ second)
        def _():
            pltpu.make_async_copy(ref_one, ref_one, sem).wait()

    def wait_rows(buf, sem, heads):
        wait_pair(
            has_up, has_down, buf.at[heads, pl.ds(0, 256)], buf.at[heads, pl.ds(0, 128)], sem
        )

    def wait_halos(buf, sem, heads):
        wait_pair(has_left, has_right, buf.at[:, :, heads], buf.at[0, :, heads], sem)

    def wait_two(buf, sem, heads, first, second):
        wait_pair(first, second, buf.at[:, heads], buf.at[0, heads], sem)

    def issue(chunk):
        kind, g = lax.div(chunk, groups), lax.rem(chunk, groups)

        @pl.when(chunk >= 0)
        def _():
            for n, copy in enumerate((q_copy, g_copy, dq_copy)):
                @pl.when(kind == n)
                def _(copy=copy):
                    for d in range(2):
                        @pl.when(vertical[d][0])
                        def _(d=d):
                            copy(d, g).start()

    def head_cols(head):
        return pl.ds(pl.multiple_of(head * LANES, LANES), LANES)

    def split(block):
        tiles = block.astype(f32).reshape(8, 2, 8, LANES)
        return [tiles[:, t].reshape(64, LANES).astype(bf16) for t in range(2)]

    def spread(ref, n):
        @pl.loop(0, HEADS)
        def _(h):
            block = ref[:, head_cols(h)]
            kv[n, h, pl.ds(0, 128)] = block
            for side, part in enumerate(split(block)):
                kv_send[side, n, h] = part

    loads[0].wait()

    def place_q(h):
        qb[h, pl.ds(128, 128)] = q_ref[:, head_cols(h)]

    for h in range(GROUP):
        place_q(h)

    pl.semaphore_wait(barrier, expected)

    issue(jnp.int32(FIRST[0]))
    loads[5].wait()
    pl.loop(GROUP, HEADS)(place_q)

    @pl.when(sec > 0)
    def _():
        sec_copy.start()

    for chunk in FIRST[1:]:
        issue(jnp.int32(chunk))

    loads[1].wait()
    spread(k_ref, 0)
    loads[2].wait()
    spread(v_ref, 1)
    for g in range(LEAD):
        start_kv(g)


    loads[3].wait()
    lane = lax.broadcasted_iota(jnp.int32, (1, LANES), 1)
    first_tile = lax.rem(lane // TILE, 2) == 0
    dead = jnp.int32(0)
    left = jnp.where(has_left, 1, 0)
    right = jnp.where(has_right, 1, 0)
    for i in range(3):
        entry = [[mask_ref[t, 3 * i + j] for j in range(3)] for t in range(2)]
        for n, (first, second) in enumerate((
            (entry[0][1], entry[1][0]),
            (entry[0][2], entry[1][1]),
            (entry[0][0] * left, dead),
            (dead, entry[1][2] * right),
        )):
            seen = jnp.where(first_tile, first, second)
            bias_send[i, pl.ds(n, 1)] = jnp.where(seen > 0, 0.0, NEG).astype(f32)
    bias[1] = bias_send[1]

    for d in range(2):
        @pl.when(vertical[d][0])
        def _(d=d):
            bias_copy(d).start()


    for cond, at in ((row == 0, 0), (row == rows_n - 1, 256)):
        @pl.when(cond)
        def _(at=at):
            bias[2 * at // 256] = jnp.zeros((4, LANES), f32)

            @pl.loop(0, HEADS)
            def _(h):
                qb[h, pl.ds(at, 128)] = jnp.zeros((128, LANES), bf16)
                gb[h, pl.ds(at, 128)] = jnp.zeros((128, LANES), bf16)
                dq_recv[at // 256, h] = jnp.zeros((128, LANES), bf16)

    for cond, side in ((col == 0, 0), (col == cols_n - 1, 1)):
        @pl.when(cond)
        def _(side=side):
            @pl.loop(0, HEADS)
            def _(h):
                for n in range(2):
                    kv[n, h, pl.ds(128 + 64 * side, 64)] = jnp.zeros((64, LANES), bf16)
                    dkv_recv[side, n, h] = jnp.zeros((64, LANES), bf16)

    stat_row = lax.broadcasted_iota(jnp.int32, (2 * GROUP, LANES), 0)
    no_stat = jnp.where(stat_row < GROUP, NEG, 0.0).astype(f32)
    for cond, pieces in (
        (row == 0, (0, 1)), (row < 2, (4,)),
        (row == rows_n - 1, (2, 3)), (row > rows_n - 3, (5,)),
    ):
        @pl.when(cond)
        def _(pieces=pieces):
            for g in range(groups):
                for piece in pieces:
                    xr1[g, piece] = no_stat

    @pl.when(sec == sections - 1)
    def _():
        handed[...] = jnp.zeros_like(handed)

    @pl.when(sec < sections - 1)
    def _():
        sec_copy.wait_recv()

    loads[4].wait()

    @pl.loop(0, HEADS)
    def _(h):
        at = head_cols(h)
        gb[h, pl.ds(128, 128)] = (c_ref[:, at].astype(f32) + handed[:, at].astype(f32)).astype(bf16)

    for chunk in SECOND:
        issue(jnp.int32(chunk))

    for g in range(LEAD):
        forward_kv(g)
        start_kv(g + LEAD)

    wait_pair(has_up, has_down, bias.at[pl.ds(0, 2)], bias.at[0], bias_sem.at[1])
    for n in range(3):
        for k in range(4):
            bias_tiles[n, k] = jnp.broadcast_to(bias[n, pl.ds(k, 1)], (8, LANES))

    nt = (((1,), (1,)), ((), ()))
    nn = (((1,), (0,)), ((), ()))
    tn = (((0,), (0,)), ((), ()))

    def dot(a, b, dims):
        return lax.dot_general(a, b, dims, preferred_element_type=f32)

    slots = [slice(n * 128, n * 128 + 128) for n in range(3)]

    def exponents(g, first, second):
        heads = pl.ds(g * GROUP, GROUP)
        wait_rows(qb, recv_q.at[g], pl.ds(0, 2 * GROUP))
        wait_halos(kv_send, recv_kv.at[g], heads)
        for i in range(GROUP):
            h = g * GROUP + i
            part = dot(kv[0, h], qb[h], nt)
            grad_part = dot(kv[1, h], gb[h], nt)
            for n, at in enumerate(slots):
                rows = part[:, at] * scale
                scores = jnp.concatenate(
                    [
                        (rows[:128].reshape(8, 2, 8, LANES) + bias_tiles[n, 0:2][None]).reshape(128, LANES),
                        (rows[128:192].reshape(8, 8, LANES) + bias_tiles[n, 2][None]).reshape(64, LANES),
                        (rows[192:].reshape(8, 8, LANES) + bias_tiles[n, 3][None]).reshape(64, LANES),
                    ],
                    axis=0,
                )
                top = jnp.max(scores, axis=0, keepdims=True)
                exps = jnp.exp2(scores - top)
                weights[h, :, at] = exps
                grads[h, :, at] = grad_part[:, at]
                total = jnp.sum(exps, axis=0, keepdims=True)
                delta = jnp.sum(exps * grad_part[:, at], axis=0, keepdims=True)
                tops[g, n, pl.ds(i, 1)] = top
                xs1[g, n, pl.ds(i, 1)] = top + jnp.log(total) * 1.4426950408889634
                xs1[g, n, pl.ds(GROUP + i, 1)] = delta / total

        stat_start(xs1, xr1, send_x1, recv_x1, g)
        issue(first)
        issue(second)

        @pl.when(g + LEAD < groups)
        def _():
            forward_kv(g + LEAD)

            @pl.when(g + 2 * LEAD < groups)
            def _():
                start_kv(g + 2 * LEAD)

    others = ((0, 4), (1, 2), (3, 5))

    def gradients(g, first, second):
        stat_wait(xr1, recv_x1.at[g], g)
        factors, deltas = [], []
        for n in range(3):
            stats = [xs1[g, n], xr1[g, others[n][0]], xr1[g, others[n][1]]]
            top = jnp.maximum(
                jnp.maximum(stats[0][:GROUP], stats[1][:GROUP]), stats[2][:GROUP]
            )
            shares = [jnp.exp2(stat[:GROUP] - top) for stat in stats]
            inverse = 1.0 / (shares[0] + shares[1] + shares[2])
            delta = sum(share * stat[GROUP:] for share, stat in zip(shares, stats))
            factors.append(jnp.exp2(tops[g, n, pl.ds(0, GROUP)] - top) * inverse)
            deltas.append(delta * inverse)
        pairs = []
        for i in range(GROUP):
            h = g * GROUP + i
            lows, scores = [], []
            for n, at in enumerate(slots):
                probs = weights[h, :, at] * factors[n][i:i + 1]
                lows.append(probs.astype(bf16))
                scores.append((probs * (grads[h, :, at] - deltas[n][i:i + 1]) * inv_root).astype(bf16))
            low = jnp.concatenate(lows, axis=1)
            score = jnp.concatenate(scores, axis=1)
            pairs.append((h, low, score))
            grad_query = dot(score, kv[0, h], tn)
            dq_send[0, h] = grad_query[:128].astype(bf16)
            dq_own[h] = grad_query[128:256]
            dq_send[1, h] = grad_query[256:].astype(bf16)

        issue(first)
        issue(second)
        for h, low, score in pairs:
            grad_value = dot(low, gb[h], nn)
            dv_own[h] = grad_value[:128]
            dkv_send[0, 1, h] = grad_value[128:192].astype(bf16)
            dkv_send[1, 1, h] = grad_value[192:].astype(bf16)
            grad_key = dot(score, qb[h], nn)
            dk_own[h] = grad_key[:128]
            dkv_send[0, 0, h] = grad_key[128:192].astype(bf16)
            dkv_send[1, 0, h] = grad_key[192:].astype(bf16)

        start_grad(g)

        @pl.when(g > 0)
        def _():
            forward_grad(g - 1)

    @pl.loop(0, len(STEPS))
    def _(t):
        stage, g, first, second = (
            sum((t == n).astype(jnp.int32) * step[at] for n, step in enumerate(STEPS))
            for at in range(4)
        )
        for n, run in enumerate((exponents, gradients)):
            @pl.when(stage == n)
            def _(run=run):
                run(g, first, second)

    def fold(own, n, h):
        blocks = own[h].reshape(8, 2, 8, LANES)
        sides = [dkv_recv[side, n, h].astype(f32).reshape(8, 1, 8, LANES) for side in range(2)]
        return (blocks + jnp.concatenate(sides, axis=1)).reshape(128, LANES).astype(bf16)

    def finish_keys(g):
        wait_halos(dkv_recv, recv_dkv.at[g], pl.ds(g * GROUP, GROUP))
        for i in range(GROUP):
            h = g * GROUP + i
            ok_ref[:, head_cols(h)] = fold(dk_own, 0, h)
            ov_ref[:, head_cols(h)] = fold(dv_own, 1, h)

    def finish_queries(g):
        heads = pl.ds(g * GROUP, GROUP)
        wait_two(dq_recv, recv_dq.at[g], heads, has_up, has_down)
        for i in range(GROUP):
            h = g * GROUP + i
            oq_ref[:, head_cols(h)] = (
                dq_own[h] + dq_recv[0, h].astype(f32) + dq_recv[1, h].astype(f32)
            ).astype(bf16)

    @pl.loop(0, groups)
    def _(g):
        finish_keys(g)
        finish_queries(g)

    @pl.when(sec > 0)
    def _():
        sec_copy.wait_send()

    every = pl.ds(0, HEADS)
    wait_pair(has_up, has_down, bias.at[pl.ds(0, 2)], bias.at[0], bias_sem.at[0])
    wait_rows(qb, send_q.at[0], every)
    wait_rows(gb, send_g.at[0], every)
    wait_two(dq_send, send_dq.at[0], every, has_up, has_down)
    stat_wait(xr1, send_x1.at[0], pl.ds(0, groups))
    wait_halos(kv_send, send_kv.at[0], every)
    wait_halos(dkv_send, send_dkv.at[0], every)
    if detour:
        for n, (names, buf) in enumerate(((VIA_KV, via_kv), (VIA_GRAD, via_dkv))):
            @pl.when(via_holder(0) | via_holder(1))
            def _(n=n, names=names, buf=buf):
                ref = buf.at[:, pl.ds(0, GROUP * len(names))]
                pltpu.make_async_copy(ref, ref, send_via.at[n]).wait()


def store_kernel(aq, ak, av, oq, ok, ov, sems):
    stores = [
        pltpu.make_async_copy(src, dst, sems.at[n])
        for n, (src, dst) in enumerate(((aq, oq), (ak, ok), (av, ov)))
    ]
    for store in stores:
        store.start()
    for store in stores:
        store.wait()


def relay_body(queries, keys, values, cotangent, upstream, block_mask):
    sections, rows_n, cols_n = (lax.axis_size(a) for a in ("section", "ha", "wa"))
    shape = queries.shape
    tokens = shape[1] * shape[2] * shape[3]
    flat = (tokens, shape[4])
    groups = HEADS // GROUP
    bf16, f32 = jnp.bfloat16, jnp.float32
    dma = pltpu.SemaphoreType.DMA
    vmem = pltpu.VMEM
    out = pl.pallas_call(
        functools.partial(relay_kernel, sections, rows_n, cols_n),
        out_shape=[vmem(flat, bf16)] * 3,
        in_specs=[pl.BlockSpec(memory_space=pltpu.HBM)] * 6,
        out_specs=[pl.BlockSpec(memory_space=pltpu.VMEM)] * 3,
        scratch_shapes=[
            vmem(flat, bf16), vmem(flat, bf16), vmem(flat, bf16), vmem(flat, bf16),
            pltpu.SMEM((2, 9), jnp.int32),
            vmem(flat, bf16),
            vmem((HEADS, 384, LANES), bf16), vmem((HEADS, 384, LANES), bf16),
            vmem((2, HEADS, 256, LANES), bf16), vmem((2, 2, HEADS, 64, LANES), bf16),
            vmem((3, 4, LANES), f32), vmem((3, 4, LANES), f32), vmem((3, 4, 8, LANES), f32),
            vmem((HEADS, 256, 384), f32), vmem((HEADS, 256, 384), f32),
            vmem((groups, 3, 8, LANES), f32),
            vmem((groups, 3, 2 * GROUP, LANES), f32), vmem((groups, 6, 2 * GROUP, LANES), f32),
            vmem((HEADS, 128, LANES), f32),
            vmem((2, HEADS, 128, LANES), bf16), vmem((2, HEADS, 128, LANES), bf16),
            vmem((HEADS, 128, LANES), f32), vmem((HEADS, 128, LANES), f32),
            vmem((2, 2, HEADS, 64, LANES), bf16), vmem((2, 2, HEADS, 64, LANES), bf16),
            vmem((2, HEADS, 64, LANES), bf16), vmem((2, HEADS, 64, LANES), bf16),
            dma((6,)), dma((2,)), dma((2,)),
            dma((1,)), dma((1,)), dma((1,)), dma((1,)), dma((1,)), dma((1,)), dma((2,)),
            dma((groups,)), dma((groups,)), dma((groups,)), dma((groups,)), dma((groups,)),
            dma((2, groups // 2)),
        ],
        compiler_params=pltpu.CompilerParams(
            collective_id=0, has_side_effects=True, vmem_limit_bytes=61 * 2**20
        ),
    )(
        queries.reshape(flat), keys.reshape(flat), values.reshape(flat),
        cotangent.reshape(flat), upstream.reshape(flat), block_mask.reshape(2, 9),
    )
    out = pl.pallas_call(
        store_kernel,
        out_shape=[jax.ShapeDtypeStruct(flat, bf16)] * 3,
        in_specs=[pl.BlockSpec(memory_space=pltpu.VMEM)] * 3,
        out_specs=[pl.BlockSpec(memory_space=pltpu.HBM)] * 3,
        scratch_shapes=[dma((3,))],
        compiler_params=pltpu.CompilerParams(vmem_limit_bytes=4 * 2**20),
    )(*out)
    return tuple(x.reshape(shape) for x in out)


def solution(mesh):
    return jax.shard_map(
        relay_body,
        mesh=mesh,
        in_specs=(
            P("section", None, "ha", "wa", None),
            P("section", None, "ha", "wa", None),
            P("section", None, "ha", "wa", None),
            P("section", None, "ha", "wa", None),
            P("section", None, "ha", "wa", None),
            P("section", "ha", "wa", None),
        ),
        out_specs=(
            P("section", None, "ha", "wa", None),
            P("section", None, "ha", "wa", None),
            P("section", None, "ha", "wa", None),
        ),
        check_vma=False,
    )
```
